32 devices in a mesh: row: 4 (over x, core), col: 8 (over z, y).
Axes of the slice: x: 2, y: 2, z: 4, core: 2. Of those that a mesh axis runs over, the one named last changes fastest.
Arguments:
- vectors: float32 [32768, 128], P(('col', 'row')), may hold values from -6 to 6
- tile_values: bfloat16 [4, 8, 22, 512, 512], P('row', 'col'), may hold values from 0 to 1
- tile_rows: int32 [4, 8, 22], P('row', 'col'), may hold values from 0 to 15, as said below
- tile_cols: int32 [4, 8, 22], P('row', 'col'), may hold values from 0 to 7
- tile_count: int32 [4, 8], P('row', 'col'), may hold values from 1 to 22, as said below
- degrees: int32 [32768], replicated, may hold values from 16 to 255
Outputs:
- result: float32 [32768, 128], P(('row', 'col'))
The draws below stay inside these ranges and needn't reach their ends.
Inputs may be any that keep to these rules, and one draw needn't show every extreme that they name: `tile_rows`: within one device no two slots name the same pair of tile row and tile column. `tile_count`: some device has all 22 slots live.
All inputs are finite; a program needn't handle non-finite values.
Results may differ from the reference program's by a relative error of at most 0.0003.
Values sent between devices are 32-bit elements; how exact they have to be, the bound alone decides.
A program may use at most 128 MiB of HBM per device.

```python
import jax
import jax.numpy as jnp
from jax import lax

TS = 512
V = 128
TILES_DEV = 22
ROW_TILES = 16
COL_TILES = 8
NODES = 32768
N_ROW = 4
N_COL = 8


def tile_places(key):
    sub_key = jax.random.fold_in(key, 7)
    dev_keys = jax.random.split(sub_key, N_ROW * N_COL)

    def pick_places(dev_key):
        return jax.random.permutation(dev_key, ROW_TILES * COL_TILES)[:TILES_DEV]
    places = jax.vmap(pick_places)(dev_keys)
    return places.reshape(N_ROW, N_COL, TILES_DEV).astype(jnp.int32)


def draw_tile_rows(key, part):
    return (tile_places(key) // COL_TILES).astype(jnp.int32)


def draw_tile_cols(key, part):
    return (tile_places(key) % COL_TILES).astype(jnp.int32)


def draw_tile_count(key, part):
    first_key, second_key = jax.random.split(jax.random.fold_in(key, 11))
    draw_base = jax.random.randint(first_key, (N_ROW * N_COL,), 0, TILES_DEV)
    counts = 1 + draw_base * draw_base // TILES_DEV
    full_device = jax.random.randint(second_key, (), 0, N_ROW * N_COL)
    flat_counts = jnp.where(jnp.arange(N_ROW * N_COL) == full_device, TILES_DEV, counts)
    return flat_counts.reshape(N_ROW, N_COL).astype(jnp.int32)


def draw_degrees(key, part):
    first_key, second_key = jax.random.split(jax.random.fold_in(key, 13))
    exponent = jax.random.randint(first_key, (NODES,), 0, 4)
    low_end = jnp.left_shift(jnp.full((NODES,), 16, jnp.int32), exponent.astype(jnp.int32))
    offset_add = jax.random.randint(second_key, (NODES,), 0, low_end)
    return (low_end + offset_add).astype(jnp.int32)


def level_of(stream_key, extent, cuts, least, largest):
    loudness, own = 1.0, jax.random.fold_in(stream_key, 6)
    for position, shards_of in cuts:
        draws = jnp.exp(jax.random.uniform(jax.random.fold_in(own, position), (shards_of,), jnp.float32, least / len(cuts), largest / len(cuts)))
        loudness = loudness * jnp.repeat(draws, extent[position] // shards_of).reshape([-1 if axis == position else 1 for axis in range(len(extent))])
    return loudness


def noise(rng, shape, spread, bound, cuts=(), kind=jnp.bfloat16):
    entries = spread * jax.random.normal(rng, shape, jnp.float32)
    if cuts:
        entries = entries * level_of(rng, shape, cuts, -0.22, 0.18)
    return jnp.clip(entries, -bound, bound).astype(kind)


def setup_inputs(seed: int = 0) -> dict:
    splits = jax.random.split(jax.random.key(seed), 7)
    vectors = noise(splits[0], (NODES, V), 1.0, 6.0, ((0, 32),), jnp.float32)
    tile_values = jnp.clip(1.0 * jax.random.uniform(splits[1], (N_ROW, N_COL, TILES_DEV, TS, TS), jnp.float32) ** level_of(splits[1], (N_ROW, N_COL, TILES_DEV, TS, TS), ((0, 4), (1, 8)), -0.2, 0.2), 0.0, 1.0).astype(jnp.bfloat16)
    tile_rows = draw_tile_rows(jax.random.fold_in(splits[6], 71), 0)
    tile_cols = draw_tile_cols(jax.random.fold_in(splits[6], 71), 0)
    tile_count = draw_tile_count(jax.random.fold_in(splits[6], 71), 0)
    degrees = draw_degrees(jax.random.fold_in(splits[6], 71), 0)
    return {"vectors": vectors, "tile_values": tile_values, "tile_rows": tile_rows, "tile_cols": tile_cols, "tile_count": tile_count, "degrees": degrees}


def reference(vectors, tile_values, tile_rows, tile_cols, tile_count, degrees):
    inv_root = lax.rsqrt(degrees.astype(jnp.float32))
    scaled = (vectors * inv_root[:, None]).reshape(NODES // TS, TS, V)
    devices = N_ROW * N_COL
    device_ids = jnp.arange(devices, dtype=jnp.int32)
    slot_ids = jnp.arange(TILES_DEV, dtype=jnp.int32)

    def add_device(summed, device_item):
        tile_block, row_ids, col_ids, live_count, device_id = device_item
        row_block = device_id // N_COL
        col_block = device_id % N_COL
        chosen = scaled[(col_block * COL_TILES + col_ids).astype(jnp.int32)]
        contrib = jnp.einsum('kij,kjv->kiv', tile_block.astype(jnp.float32), chosen.astype(jnp.float32), precision=lax.Precision.HIGHEST)
        live_mask = (slot_ids < live_count).astype(jnp.float32)
        contrib = contrib * live_mask[:, None, None]
        summed = summed.at[(row_block * ROW_TILES + row_ids).astype(jnp.int32)].add(contrib)
        return (summed, None)
    start = jnp.zeros((NODES // TS, TS, V), jnp.float32)
    summed, _ = lax.scan(add_device, start, (tile_values.reshape(devices, TILES_DEV, TS, TS), tile_rows.reshape(devices, TILES_DEV), tile_cols.reshape(devices, TILES_DEV), tile_count.reshape(devices), device_ids))
    return summed.reshape(NODES, V) * inv_root[:, None]
```

```python
import functools

import jax
import jax.numpy as jnp
from jax import lax
from jax.experimental import pallas as pl
from jax.experimental.pallas import tpu as pltpu
from jax.sharding import PartitionSpec as P

MESH = pl.DeviceIdType.MESH
LANES = 128
SLICES = 4
CHUNK = 32


def inner_size(col_count):
    inner = 1
    while inner * inner * 4 <= col_count and col_count % (inner * 2) == 0:
        inner *= 2
    return inner


def sorted_table(count):
    return [sorted(range(count), key=lambda d: (-abs(d - i), -d)) for i in range(count)]


def tail_rows(packed):
    return (packed // 2, packed // 4) + (0,) * (SLICES - 2)


def kernel(
    dims,
    rows_s, cols_s, count_s, vec_hbm, deg_hbm, tiles_hbm, out_ref,
    tiles_v, vec_v, deg_v, fin, fout, gath, rhs, sums, part, inb, outb, zb, yb, prev_s, last_s,
    tile_sem, vec_sem, deg_sem, d_send, d_recv, m_send, m_recv, f_send, f_recv,
    i_send, i_recv, o_send, o_recv, z_send, z_recv, y_send, y_recv,
):
    R, A, B, piece, width, side, slots = dims
    C = A * B
    S = SLICES
    gw = width // S
    packed = piece // S
    tpp = piece // side
    halves = S // tpp
    blocks = packed // LANES
    tails = tail_rows(packed)
    tailed = [s for s in range(S) if tails[s]]
    chips = R // 2
    me_row = lax.axis_index("row")
    me_col = lax.axis_index("col")
    chip, core = me_row // 2, me_row % 2
    mate = chip * 2 + (1 - core)
    a, b = me_col // B, me_col % B
    f32 = jnp.float32

    def rdma(src, dst, ssem, rsem, where):
        return pltpu.make_async_remote_copy(
            src_ref=src, dst_ref=dst, send_sem=ssem, recv_sem=rsem,
            device_id=where, device_id_type=MESH,
        )

    vec_copy = pltpu.make_async_copy(vec_hbm, vec_v, vec_sem)
    vec_copy.start()
    deg_n = piece // LANES
    deg_at = (me_col * R + me_row, me_row * C + me_col)
    deg_copies = []
    for i, at in enumerate(deg_at):
        cp = pltpu.make_async_copy(
            deg_hbm.at[pl.ds(pl.multiple_of(at * deg_n, deg_n), deg_n)], deg_v.at[i], deg_sem.at[i])
        cp.start()
        deg_copies.append(cp)
    tile_copy = pltpu.make_async_copy(tiles_hbm.at[0, 0], tiles_v, tile_sem)
    tile_copy.start()

    barrier = pltpu.get_barrier_semaphore()

    def greet(where):
        pl.semaphore_signal(barrier, inc=1, device_id=where, device_id_type=MESH)

    greet({"row": mate})
    for j in range(1, chips):
        greet({"row": lax.rem(chip + j, chips) * 2 + core})
    conds = []
    if B > 1:
        conds += [(b > 0, me_col - 1), (b < B - 1, me_col + 1)]
    if A > 1:
        conds += [(a > 0, me_col - B), (a < A - 1, me_col + B)]
    for cond, other in conds:
        @pl.when(cond)
        def _(other=other):
            greet({"col": other})
    peers = jnp.int32(chips)
    for cond, other in conds:
        peers = peers + jnp.where(cond, 1, 0)

    group = lax.broadcasted_iota(jnp.int32, (CHUNK, LANES), 1) // gw
    odd = group % 2 == 1

    def place(q):
        u, h = q // halves, q % halves
        return u, h

    def first_row(blk, h):
        return (blk * halves + h) * LANES

    def by_group(values):
        out = values[S - 1]
        for g in range(S - 2, -1, -1):
            out = jnp.where(group == g, values[g], out)
        return out

    def roll(x, steps):
        steps = steps % S
        return pltpu.roll(x, steps * gw, 1) if steps else x

    for cp in deg_copies:
        cp.wait()
    for i, ref in enumerate((fin, fout)):
        f = lax.rsqrt(deg_v[i].astype(f32))
        for blk in range(blocks):
            rows = []
            for q in range(S):
                u, h = place(q)
                at = u * (side // LANES) + blk * halves + h
                rows.append(jnp.broadcast_to(f[at:at + 1, :], (gw, LANES)))
            ref[blk * LANES:(blk + 1) * LANES, :] = jnp.concatenate(rows, 0).T

    vec_copy.wait()
    for blk in range(blocks):
        def pack_own(c, _, blk=blk):
            at = pl.multiple_of(c * CHUNK, CHUNK)
            v = []
            for q in range(S):
                u, h = place(q)
                v.append(vec_v[pl.ds(u * side + first_row(blk, h) + at, CHUNK)])
            to = pl.ds(blk * LANES + at, CHUNK)
            f = fin[to]
            for s in range(S):
                x = by_group([roll(v[q], q - s) for q in range(S)])
                gath[s, me_row, to] = x * f
            return 0

        lax.fori_loop(0, LANES // CHUNK, pack_own, 0)

    pl.semaphore_wait(barrier, peers)

    directs, mates, forwards = {}, {}, {}
    for s in range(S):
        for j in range(1, chips):
            dst = lax.rem(chip + j, chips) * 2 + core
            cp = rdma(gath.at[s, me_row], gath.at[s, me_row],
                      d_send.at[j - 1, s], d_recv.at[j - 1, s], {"row": dst})
            cp.start()
            directs[j, s] = cp
        cp = rdma(gath.at[s, me_row], gath.at[s, me_row],
                  m_send.at[s], m_recv.at[s], {"row": mate})
        cp.start()
        mates[s] = cp

    count = count_s[0, 0]

    def link(k, _):
        rk = rows_s[0, 0, k]
        v = jnp.int32(slots)
        for j in range(slots):
            v = jnp.where((rows_s[0, 0, j] == rk) & (j < k), j, v)
        prev_s[k] = v
        return 0

    def ends(r, _):
        v = jnp.int32(slots)
        for j in range(slots):
            v = jnp.where((rows_s[0, 0, j] == r) & (j < count), j, v)
        last_s[r] = v
        return 0

    def landed(s, r, ssem, rsem):
        rdma(gath.at[s, r], gath.at[s, r], ssem, rsem, {"row": mate}).wait_recv()

    def operand(s, r):
        for blk in range(blocks):
            def step(c, _, blk=blk):
                at = pl.multiple_of(c * CHUNK, CHUNK)
                x = gath[s, r, pl.ds(blk * LANES + at, CHUNK)]
                turned = [roll(x, n) for n in range(S)]
                for q in range(S):
                    u, h = place(q)
                    rep = by_group([turned[(g - q) % S] for g in range(S)])
                    hi = rep.astype(jnp.bfloat16).astype(f32)
                    v = jnp.where(odd, rep - hi, hi)
                    rhs[r * tpp + u, pl.ds(first_row(blk, h) + at, CHUNK), :] = v.astype(jnp.bfloat16)
                return 0

            lax.fori_loop(0, LANES // CHUNK, step, 0)

    def forward(s):
        for j in range(1, chips):
            src = lax.rem(chip - j + chips, chips) * 2 + core
            landed(s, src, d_send.at[j - 1, s], d_recv.at[j - 1, s])
            cp = rdma(gath.at[s, src], gath.at[s, src],
                      f_send.at[j - 1, s], f_recv.at[j - 1, s], {"row": mate})
            cp.start()
            forwards[j, s] = cp

    def operands_own(s):
        operand(s, me_row)
        landed(s, mate, m_send.at[s], m_recv.at[s])
        operand(s, mate)

    def operands_far(s):
        for j in range(1, chips):
            operand(s, lax.rem(chip - j + chips, chips) * 2 + core)
        for j in range(1, chips):
            src = lax.rem(chip - j + chips, chips) * 2 + (1 - core)
            landed(s, src, f_send.at[j - 1, s], f_recv.at[j - 1, s])
            operand(s, src)

    def products(lo, n):
        def product(k, _):
            both = jnp.dot(tiles_v[k, lo:lo + n], rhs[cols_s[0, 0, k]],
                           preferred_element_type=f32)
            sums[k, lo:lo + n] = both + sums[prev_s[k], lo:lo + n]
            return 0

        lax.fori_loop(0, slots, product, 0, unroll=True)

    def pack(s, blk):
        def step(dest, _):
            for c in range(0, LANES, CHUNK):
                v = []
                for q in range(S):
                    u, h = place(q)
                    at = first_row(blk, h) + c
                    v.append(sums[last_s[dest * tpp + u], at:at + CHUNK])
                x = by_group(v)
                y = by_group([v[(g + 1) % S] for g in range(S)])
                at = blk * LANES + c
                part[s, dest, at:at + CHUNK] = x + roll(y, 1)
            return 0

        lax.fori_loop(0, C, step, 0)

    order = sorted_table(A)

    def pick(i):
        v = jnp.int32(order[0][i])
        for n in range(1, A):
            v = jnp.where(a == n, order[n][i], v)
        return v

    def line(pos, size, stride, dist, action):
        for right in (True, False):
            t = pos + dist if right else pos - dist
            slot = t + 1 if right else t
            to = me_col + stride if right else me_col - stride
            more = pos > 0 if right else pos < size - 1

            @pl.when((t < size) if right else (t >= 0))
            def _(t=t, slot=slot, to=to, more=more):
                action(t, slot, to, more, dist < size - 1)

    def arrive(pos, size, ref, ssem, rsem, fold):
        if size > 1:
            for cond, slot in ((pos > 0, pos + 1), (pos < size - 1, pos)):
                @pl.when(cond)
                def _(slot=slot):
                    rdma(ref(slot), ref(slot), ssem(slot), rsem(slot), {"row": mate}).wait_recv()
        if size > 2:
            @pl.when((pos > 0) & (pos < size - 1))
            def _():
                fold(pos + 1, pos)

    near = jnp.where(b > 0, b + 1, 0)
    near_a = jnp.where(a > 0, a + 1, 0)

    def rest(s):
        return pl.ds(tails[s], packed - tails[s])

    def inner_copy(s, d, t, slot, to):
        return rdma(part.at[s, d * B + t, rest(s)], inb.at[s, d, slot, rest(s)],
                    i_send.at[s, d, slot], i_recv.at[s, d, slot], {"col": to})

    def inner_send(s, i):
        d = pick(i)

        def action(t, slot, to, more, can):
            cp = inner_copy(s, d, t, slot, to)
            if can:
                @pl.when(more)
                def _():
                    cp.wait_recv()
                    at = rest(s)
                    part[s, d * B + t, at] = part[s, d * B + t, at] + inb[s, d, slot, at]
            cp.start()

        for dist in range(B - 1, 0, -1):
            line(b, B, 1, dist, action)

    def inner_done(s, d):
        at = rest(s)

        def fold(x, y):
            inb[s, d, x, at] = inb[s, d, x, at] + inb[s, d, y, at]

        arrive(b, B, lambda q: inb.at[s, d, q, at], lambda q: i_send.at[s, d, q],
               lambda q: i_recv.at[s, d, q], fold)

    def here(s, d, at):
        v = part[s, d * B + b, at]
        if B > 1:
            v = v + inb[s, d, near, at]
        return v

    def outer_copy(s, i):
        d = pick(i)
        right = d > a
        slot = jnp.where(right, d + 1, d)
        to = jnp.where(right, me_col + B, me_col - B)
        more = (right & (a > 0)) | (jnp.logical_not(right) & (a < A - 1))
        cp = rdma(part.at[s, d * B + b, rest(s)], outb.at[s, slot, rest(s)],
                  o_send.at[s, slot], o_recv.at[s, slot], {"col": to})
        return d, slot, more, cp

    def outer_step(s, i, now):
        d, slot, more, cp = outer_copy(s, i)
        at = rest(s)
        if now:
            @pl.when(jnp.logical_not(more))
            def _():
                inner_done(s, d)
                part[s, d * B + b, at] = here(s, d, at)
                cp.start()
        else:
            @pl.when(more)
            def _():
                inner_done(s, d)
                cp.wait_recv()
                part[s, d * B + b, at] = here(s, d, at) + outb[s, slot, at]
                cp.start()

    def tail_copy(s, d, slot, to):
        rows = pl.ds(0, tails[s])
        return rdma(part.at[s, pl.ds(d * B, B), rows], zb.at[s, slot, :, rows],
                    z_send.at[s, slot], z_recv.at[s, slot], {"col": to})

    def tail_send(s, dist, now):
        rows = pl.ds(0, tails[s])

        def action(d, slot, to, more, can):
            cp = tail_copy(s, d, slot, to)
            if now:
                @pl.when(jnp.logical_not(more))
                def _():
                    cp.start()
            elif can:
                @pl.when(more)
                def _():
                    cp.wait_recv()
                    for t in range(B):
                        part[s, d * B + t, rows] = part[s, d * B + t, rows] + zb[s, slot, t, rows]
                    cp.start()

        line(a, A, B, dist, action)

    def turn_copy(s, t, slot, to):
        rows = pl.ds(0, tails[s])
        return rdma(part.at[s, a * B + t, rows], yb.at[s, slot, rows],
                    y_send.at[s, slot], y_recv.at[s, slot], {"col": to})

    def turn(s):
        rows = pl.ds(0, tails[s])

        def fold(x, y):
            zb[s, x, :, rows] = zb[s, x, :, rows] + zb[s, y, :, rows]

        arrive(a, A, lambda q: zb.at[s, q, :, rows], lambda q: z_send.at[s, q],
               lambda q: z_recv.at[s, q], fold)

        def action(t, slot, to, more, can):
            cp = turn_copy(s, t, slot, to)
            v = part[s, a * B + t, rows]
            if A > 1:
                v = v + zb[s, near_a, t, rows]
            part[s, a * B + t, rows] = v
            if can:
                @pl.when(more)
                def _():
                    cp.wait_recv()
                    part[s, a * B + t, rows] = part[s, a * B + t, rows] + yb[s, slot, rows]
            cp.start()

        for dist in range(B - 1, 0, -1):
            line(b, B, 1, dist, action)

    def write(s, lo, hi, get):
        for at in range(lo, hi, CHUNK):
            blk, c = at // LANES, at % LANES
            total = get(pl.ds(at, CHUNK)) * fout[at:at + CHUNK]
            for q in range(S):
                u, h = place(q)
                to = u * side + first_row(blk, h) + c
                out_ref[to:to + CHUNK, s * gw:(s + 1) * gw] = roll(total, s - q)[:, s * gw:(s + 1) * gw]

    def finish(s):
        at = rest(s)
        inner_done(s, a)
        if A > 1:
            def fold(x, y):
                outb[s, x, at] = outb[s, x, at] + outb[s, y, at]

            arrive(a, A, lambda q: outb.at[s, q, at], lambda q: o_send.at[s, q],
                   lambda q: o_recv.at[s, q], fold)

        def get(rows):
            v = here(s, a, rows)
            if A > 1:
                v = v + outb[s, near_a, rows]
            return v

        write(s, tails[s], packed, get)

    def finish_tail(s):
        rows = pl.ds(0, tails[s])

        def fold(x, y):
            yb[s, x, rows] = yb[s, x, rows] + yb[s, y, rows]

        arrive(b, B, lambda q: yb.at[s, q, rows], lambda q: y_send.at[s, q],
               lambda q: y_recv.at[s, q], fold)

        def get(rows):
            v = part[s, a * B + b, rows]
            if A > 1:
                v = v + zb[s, near_a, b, rows]
            if B > 1:
                v = v + yb[s, near, rows]
            return v

        write(s, 0, tails[s], get)

    lax.fori_loop(0, slots, link, 0)
    lax.fori_loop(0, C * tpp, ends, 0)
    sums[slots] = jnp.zeros((side, LANES), f32)

    def all_tails(s, now, dists):
        if A > 1:
            for dist in dists:
                tail_send(s, dist, now)

    every = range(A - 1, 0, -1)

    operands_own(0)
    forward(0)
    operands_far(0)
    tile_copy.wait()
    span = side // blocks
    for blk in range(blocks):
        products(blk * span, span)
        pack(0, blk)
        if blk == 0:
            all_tails(0, True, every)
            forward(1)
    for i in range(A):
        inner_send(0, i)
    forward(2)
    operands_own(1)
    operands_far(1)
    products(0, side)
    for blk in range(blocks):
        pack(1, blk)
    all_tails(1, True, every)
    for i in range(A):
        inner_send(1, i)
    all_tails(0, False, list(every)[:-1])
    forward(3)
    operands_own(2)
    operands_far(2)
    products(0, side)
    for blk in range(blocks):
        pack(2, blk)
    inner_send(2, 0)
    for i in range(A - 1):
        outer_step(0, i, True)
    all_tails(0, False, list(every)[-1:])
    operands_own(3)
    operands_far(3)
    products(0, side)
    for blk in range(blocks):
        pack(3, blk)
    inner_send(3, 0)
    for i in range(1, A):
        inner_send(2, i)
        inner_send(3, i)
    all_tails(1, False, every)
    for s in (0, 1):
        for i in range(A - 1):
            if s > 0:
                outer_step(s, i, True)
            outer_step(s, i, False)
    turn(0)
    turn(1)
    for i in range(A - 1):
        for s in (2, 3):
            outer_step(s, i, True)
            outer_step(s, i, False)
        if i < 2:
            finish(i)
    for s in range(min(2, A - 1), S):
        finish(s)
    for s in tailed:
        finish_tail(s)

    for sent in (directs.values(), mates.values(), forwards.values()):
        for cp in sent:
            cp.wait_send()
    for s in tailed:
        for dist in every:
            line(a, A, B, dist, lambda d, slot, to, *rest, s=s: tail_copy(s, d, slot, to).wait_send())
        for dist in range(B - 1, 0, -1):
            line(b, B, 1, dist, lambda t, slot, to, *rest, s=s: turn_copy(s, t, slot, to).wait_send())
    for s in range(S):
        for i in range(A):
            for dist in range(B - 1, 0, -1):
                def left(t, slot, to, *rest, s=s, d=pick(i)):
                    inner_copy(s, d, t, slot, to).wait_send()

                line(b, B, 1, dist, left)
        for i in range(A - 1):
            outer_copy(s, i)[-1].wait_send()


def body(vectors, tile_values, tile_rows, tile_cols, tile_count, degrees):
    R = lax.axis_size("row")
    C = lax.axis_size("col")
    piece, width = vectors.shape
    side = tile_values.shape[-1]
    slots = tile_values.shape[2]
    B = inner_size(C)
    A = C // B
    tpp = piece // side
    chips = R // 2
    dims = (R, A, B, piece, width, side, slots)
    vmem = pl.BlockSpec(memory_space=pltpu.VMEM)
    smem = pl.BlockSpec(memory_space=pltpu.SMEM)
    anywhere = pl.BlockSpec(memory_space=pl.ANY)
    dma = pltpu.SemaphoreType.DMA
    f32 = jnp.float32
    far = max(chips - 1, 1)
    S = SLICES
    packed = piece // S
    tails = tail_rows(packed)
    kinds = sum(1 for n in tails if n)
    return pl.pallas_call(
        functools.partial(kernel, dims),
        out_shape=jax.ShapeDtypeStruct((piece, width), f32),
        in_specs=[smem, smem, smem, anywhere, anywhere, anywhere],
        out_specs=vmem,
        scratch_shapes=[
            pltpu.VMEM((slots, side, side), tile_values.dtype),
            pltpu.VMEM((piece, width), f32),
            pltpu.VMEM((2, piece // LANES, LANES), jnp.int32),
            pltpu.VMEM((packed, LANES), f32),
            pltpu.VMEM((packed, LANES), f32),
            pltpu.VMEM((S, R, packed, LANES), f32),
            pltpu.VMEM((R * tpp, side, LANES), jnp.bfloat16),
            pltpu.VMEM((slots + 1, side, LANES), f32),
            pltpu.VMEM((S, C, packed, LANES), f32),
            pltpu.VMEM((S, A, B + 1, packed, LANES), f32),
            pltpu.VMEM((S, A + 1, packed, LANES), f32),
            pltpu.VMEM((kinds, A + 1, B, max(tails), LANES), f32),
            pltpu.VMEM((kinds, B + 1, max(tails), LANES), f32),
            pltpu.SMEM((slots,), jnp.int32),
            pltpu.SMEM((C * tpp,), jnp.int32),
            dma, dma, dma((2,)),
            dma((far, S)), dma((far, S)),
            dma((S,)), dma((S,)),
            dma((far, S)), dma((far, S)),
            dma((S, A, B + 1)), dma((S, A, B + 1)),
            dma((S, A + 1)), dma((S, A + 1)),
            dma((kinds, A + 1)), dma((kinds, A + 1)),
            dma((kinds, B + 1)), dma((kinds, B + 1)),
        ],
        compiler_params=pltpu.CompilerParams(
            collective_id=0, has_side_effects=True, vmem_limit_bytes=67043328
        ),
    )(tile_rows, tile_cols, tile_count, vectors, degrees.reshape(-1, LANES), tile_values)


def solution(mesh):
    placed = (
        P(("col", "row"), None),
        P("row", "col", None, None, None),
        P("row", "col", None),
        P("row", "col", None),
        P("row", "col"),
        P(),
    )
    return jax.shard_map(
        body, mesh=mesh, in_specs=placed, out_specs=P(("row", "col"), None), check_vma=False
    )
```

```python
import functools

import jax
import jax.numpy as jnp
from jax import lax
from jax.experimental import pallas as pl
from jax.experimental.pallas import tpu as pltpu
from jax.sharding import PartitionSpec as P

MESH = pl.DeviceIdType.MESH
LANES = 128
SLICES = 4
CHUNK = 32


def inner_size(col_count):
    inner = 1
    while inner * inner * 4 <= col_count and col_count % (inner * 2) == 0:
        inner *= 2
    return inner


def sorted_table(count):
    return [sorted(range(count), key=lambda d: (-abs(d - i), -d)) for i in range(count)]


def tail_rows(packed):
    return (packed // 2, packed // 4) + (0,) * (SLICES - 2)


def kernel(
    dims,
    rows_s, cols_s, count_s, vec_hbm, deg_hbm, tiles_hbm, out_ref,
    tiles_v, vec_v, deg_v, fin, fout, gath, rhs, sums, part, inb, outb, zb, yb, prev_s, last_s,
    tile_sem, vec_sem, deg_sem, d_send, d_recv, m_send, m_recv, f_send, f_recv,
    i_send, i_recv, o_send, o_recv, z_send, z_recv, y_send, y_recv,
):
    R, A, B, piece, width, side, slots = dims
    C = A * B
    S = SLICES
    gw = width // S
    packed = piece // S
    tpp = piece // side
    halves = S // tpp
    blocks = packed // LANES
    tails = tail_rows(packed)
    tailed = [s for s in range(S) if tails[s]]
    chips = R // 2
    me_row = lax.axis_index("row")
    me_col = lax.axis_index("col")
    chip, core = me_row // 2, me_row % 2
    mate = chip * 2 + (1 - core)
    a, b = me_col // B, me_col % B
    f32 = jnp.float32

    def rdma(src, dst, ssem, rsem, where):
        return pltpu.make_async_remote_copy(
            src_ref=src, dst_ref=dst, send_sem=ssem, recv_sem=rsem,
            device_id=where, device_id_type=MESH,
        )

    vec_copy = pltpu.make_async_copy(vec_hbm, vec_v, vec_sem)
    vec_copy.start()
    deg_n = piece // LANES
    deg_at = (me_col * R + me_row, me_row * C + me_col)
    deg_copies = []
    for i, at in enumerate(deg_at):
        cp = pltpu.make_async_copy(
            deg_hbm.at[pl.ds(pl.multiple_of(at * deg_n, deg_n), deg_n)], deg_v.at[i], deg_sem.at[i])
        cp.start()
        deg_copies.append(cp)
    tile_copy = pltpu.make_async_copy(tiles_hbm.at[0, 0], tiles_v, tile_sem)
    tile_copy.start()

    barrier = pltpu.get_barrier_semaphore()

    def greet(where):
        pl.semaphore_signal(barrier, inc=1, device_id=where, device_id_type=MESH)

    greet({"row": mate})
    for j in range(1, chips):
        greet({"row": lax.rem(chip + j, chips) * 2 + core})
    conds = []
    if B > 1:
        conds += [(b > 0, me_col - 1), (b < B - 1, me_col + 1)]
    if A > 1:
        conds += [(a > 0, me_col - B), (a < A - 1, me_col + B)]
    for cond, other in conds:
        @pl.when(cond)
        def _(other=other):
            greet({"col": other})
    peers = jnp.int32(chips)
    for cond, other in conds:
        peers = peers + jnp.where(cond, 1, 0)

    group = lax.broadcasted_iota(jnp.int32, (CHUNK, LANES), 1) // gw
    odd = group % 2 == 1

    def place(q):
        u, h = q // halves, q % halves
        return u, h

    def first_row(blk, h):
        return (blk * halves + h) * LANES

    def by_group(values):
        out = values[S - 1]
        for g in range(S - 2, -1, -1):
            out = jnp.where(group == g, values[g], out)
        return out

    def roll(x, steps):
        steps = steps % S
        return pltpu.roll(x, steps * gw, 1) if steps else x

    for cp in deg_copies:
        cp.wait()
    for i, ref in enumerate((fin, fout)):
        f = lax.rsqrt(deg_v[i].astype(f32))
        for blk in range(blocks):
            rows = []
            for q in range(S):
                u, h = place(q)
                at = u * (side // LANES) + blk * halves + h
                rows.append(jnp.broadcast_to(f[at:at + 1, :], (gw, LANES)))
            ref[blk * LANES:(blk + 1) * LANES, :] = jnp.concatenate(rows, 0).T

    def pack_own(s):
        for blk in range(blocks):
            for c in range(0, LANES, CHUNK):
                v = []
                for q in range(S):
                    u, h = place(q)
                    at = u * side + first_row(blk, h) + c
                    v.append(roll(vec_v[at:at + CHUNK], q - s))
                to = blk * LANES + c
                gath[s, me_row, to:to + CHUNK] = by_group(v) * fin[to:to + CHUNK]

    directs, mates, forwards = {}, {}, {}

    def send_own(s):
        for j in range(1, chips):
            dst = lax.rem(chip + j, chips) * 2 + core
            cp = rdma(gath.at[s, me_row], gath.at[s, me_row],
                      d_send.at[j - 1, s], d_recv.at[j - 1, s], {"row": dst})
            cp.start()
            directs[j, s] = cp
        cp = rdma(gath.at[s, me_row], gath.at[s, me_row],
                  m_send.at[s], m_recv.at[s], {"row": mate})
        cp.start()
        mates[s] = cp

    vec_copy.wait()
    pack_own(0)
    pl.semaphore_wait(barrier, peers)
    send_own(0)
    for s in range(1, S):
        pack_own(s)
        send_own(s)

    count = count_s[0, 0]

    def link(k, _):
        rk = rows_s[0, 0, k]
        v = jnp.int32(slots)
        for j in range(slots):
            v = jnp.where((rows_s[0, 0, j] == rk) & (j < k), j, v)
        prev_s[k] = v
        return 0

    def ends(r, _):
        v = jnp.int32(slots)
        for j in range(slots):
            v = jnp.where((rows_s[0, 0, j] == r) & (j < count), j, v)
        last_s[r] = v
        return 0

    def landed(s, r, ssem, rsem):
        rdma(gath.at[s, r], gath.at[s, r], ssem, rsem, {"row": mate}).wait_recv()

    low = group < S // 2

    def operand(s, r, lane):
        for blk in range(blocks):
            for c in range(0, LANES, CHUNK):
                at = blk * LANES + c
                x = gath[s, r, at:at + CHUNK]
                hi = x.astype(jnp.bfloat16).astype(f32)
                lo = x - hi
                same, swapped = jnp.where(odd, lo, hi), jnp.where(odd, hi, lo)
                t = (same, roll(swapped, 1), roll(same, 2), roll(swapped, 3))
                e, f = jnp.where(odd, t[1], t[0]), jnp.where(odd, t[3], t[2])
                g, k = jnp.where(odd, t[0], t[3]), jnp.where(odd, t[2], t[1])
                spread = (jnp.where(low, e, f), jnp.where(low, g, k),
                          jnp.where(low, f, e), jnp.where(low, k, g))
                for q in range(S):
                    u, h = place(q)
                    to = first_row(blk, h) + c
                    rhs[r * tpp + u, to:to + CHUNK, lane:lane + LANES] = spread[q].astype(jnp.bfloat16)

    def forward(s):
        for j in range(1, chips):
            src = lax.rem(chip - j + chips, chips) * 2 + core
            landed(s, src, d_send.at[j - 1, s], d_recv.at[j - 1, s])
            cp = rdma(gath.at[s, src], gath.at[s, src],
                      f_send.at[j - 1, s], f_recv.at[j - 1, s], {"row": mate})
            cp.start()
            forwards[j, s] = cp

    def arrivals(s):
        landed(s, mate, m_send.at[s], m_recv.at[s])
        for j in range(1, chips):
            src = lax.rem(chip - j + chips, chips) * 2 + (1 - core)
            landed(s, src, f_send.at[j - 1, s], f_recv.at[j - 1, s])

    def operands(s, lane):
        def step(r, _):
            operand(s, r, lane)
            return 0

        lax.fori_loop(0, R, step, 0)

    span = side // blocks

    def products(blk, lanes):
        def product(k, _):
            both = jnp.dot(tiles_v[k, blk * span:(blk + 1) * span], rhs[cols_s[0, 0, k], :, :lanes],
                           preferred_element_type=f32)
            sums[k, :, :lanes] = both + sums[prev_s[k], :, :lanes]
            return 0

        lax.fori_loop(0, slots, product, 0, unroll=True)

    def pack(s, blk, lane):
        def step(dest, _):
            for c in range(0, LANES, CHUNK):
                v = []
                for q in range(S):
                    u, h = place(q)
                    at = h * LANES + c
                    v.append(sums[last_s[dest * tpp + u], at:at + CHUNK, lane:lane + LANES])
                x = by_group(v)
                y = by_group([v[(g + 1) % S] for g in range(S)])
                at = blk * LANES + c
                part[s, dest, at:at + CHUNK] = x + roll(y, 1)
            return 0

        lax.fori_loop(0, C, step, 0, unroll=4)

    order = sorted_table(A)

    def pick(i):
        v = jnp.int32(order[0][i])
        for n in range(1, A):
            v = jnp.where(a == n, order[n][i], v)
        return v

    def line(pos, size, stride, dist, action):
        for right in (True, False):
            t = pos + dist if right else pos - dist
            slot = t + 1 if right else t
            to = me_col + stride if right else me_col - stride
            more = pos > 0 if right else pos < size - 1

            @pl.when((t < size) if right else (t >= 0))
            def _(t=t, slot=slot, to=to, more=more):
                action(t, slot, to, more, dist < size - 1)

    def arrive(pos, size, ref, ssem, rsem, fold):
        if size > 1:
            for cond, slot in ((pos > 0, pos + 1), (pos < size - 1, pos)):
                @pl.when(cond)
                def _(slot=slot):
                    rdma(ref(slot), ref(slot), ssem(slot), rsem(slot), {"row": mate}).wait_recv()
        if size > 2:
            @pl.when((pos > 0) & (pos < size - 1))
            def _():
                fold(pos + 1, pos)

    near = jnp.where(b > 0, b + 1, 0)
    near_a = jnp.where(a > 0, a + 1, 0)

    def rest(s):
        return pl.ds(tails[s], packed - tails[s])

    def inner_copy(s, d, t, slot, to):
        return rdma(part.at[s, d * B + t, rest(s)], inb.at[s, d, slot, rest(s)],
                    i_send.at[s, d, slot], i_recv.at[s, d, slot], {"col": to})

    def inner_send(s, i):
        d = pick(i)

        def action(t, slot, to, more, can):
            cp = inner_copy(s, d, t, slot, to)
            if can:
                @pl.when(more)
                def _():
                    cp.wait_recv()
                    at = rest(s)
                    part[s, d * B + t, at] = part[s, d * B + t, at] + inb[s, d, slot, at]
            cp.start()

        for dist in range(B - 1, 0, -1):
            line(b, B, 1, dist, action)

    def inner_done(s, d):
        at = rest(s)

        def fold(x, y):
            inb[s, d, x, at] = inb[s, d, x, at] + inb[s, d, y, at]

        arrive(b, B, lambda q: inb.at[s, d, q, at], lambda q: i_send.at[s, d, q],
               lambda q: i_recv.at[s, d, q], fold)

    def here(s, d, at):
        v = part[s, d * B + b, at]
        if B > 1:
            v = v + inb[s, d, near, at]
        return v

    def outer_copy(s, i):
        d = pick(i)
        right = d > a
        slot = jnp.where(right, d + 1, d)
        to = jnp.where(right, me_col + B, me_col - B)
        more = (right & (a > 0)) | (jnp.logical_not(right) & (a < A - 1))
        cp = rdma(part.at[s, d * B + b, rest(s)], outb.at[s, slot, rest(s)],
                  o_send.at[s, slot], o_recv.at[s, slot], {"col": to})
        return d, slot, more, cp

    def outer_step(s, i, now):
        d, slot, more, cp = outer_copy(s, i)
        at = rest(s)
        if now:
            @pl.when(jnp.logical_not(more))
            def _():
                inner_done(s, d)
                part[s, d * B + b, at] = here(s, d, at)
                cp.start()
        else:
            @pl.when(more)
            def _():
                inner_done(s, d)
                cp.wait_recv()
                part[s, d * B + b, at] = here(s, d, at) + outb[s, slot, at]
                cp.start()

    def tail_copy(s, d, slot, to):
        rows = pl.ds(0, tails[s])
        return rdma(part.at[s, pl.ds(d * B, B), rows], zb.at[s, slot, :, rows],
                    z_send.at[s, slot], z_recv.at[s, slot], {"col": to})

    def tail_send(s, dist, now):
        rows = pl.ds(0, tails[s])

        def action(d, slot, to, more, can):
            cp = tail_copy(s, d, slot, to)
            if now:
                @pl.when(jnp.logical_not(more))
                def _():
                    cp.start()
            elif can:
                @pl.when(more)
                def _():
                    cp.wait_recv()
                    for t in range(B):
                        part[s, d * B + t, rows] = part[s, d * B + t, rows] + zb[s, slot, t, rows]
                    cp.start()

        line(a, A, B, dist, action)

    def turn_copy(s, t, slot, to):
        rows = pl.ds(0, tails[s])
        return rdma(part.at[s, a * B + t, rows], yb.at[s, slot, rows],
                    y_send.at[s, slot], y_recv.at[s, slot], {"col": to})

    def turn(s):
        rows = pl.ds(0, tails[s])

        def fold(x, y):
            zb[s, x, :, rows] = zb[s, x, :, rows] + zb[s, y, :, rows]

        arrive(a, A, lambda q: zb.at[s, q, :, rows], lambda q: z_send.at[s, q],
               lambda q: z_recv.at[s, q], fold)

        def action(t, slot, to, more, can):
            cp = turn_copy(s, t, slot, to)
            v = part[s, a * B + t, rows]
            if A > 1:
                v = v + zb[s, near_a, t, rows]
            part[s, a * B + t, rows] = v
            if can:
                @pl.when(more)
                def _():
                    cp.wait_recv()
                    part[s, a * B + t, rows] = part[s, a * B + t, rows] + yb[s, slot, rows]
            cp.start()

        for dist in range(B - 1, 0, -1):
            line(b, B, 1, dist, action)

    def write(s, lo, hi, get):
        for at in range(lo, hi, CHUNK):
            blk, c = at // LANES, at % LANES
            total = get(pl.ds(at, CHUNK)) * fout[at:at + CHUNK]
            for q in range(S):
                u, h = place(q)
                to = u * side + first_row(blk, h) + c
                out_ref[to:to + CHUNK, s * gw:(s + 1) * gw] = roll(total, s - q)[:, s * gw:(s + 1) * gw]

    def finish(s):
        at = rest(s)
        inner_done(s, a)
        if A > 1:
            def fold(x, y):
                outb[s, x, at] = outb[s, x, at] + outb[s, y, at]

            arrive(a, A, lambda q: outb.at[s, q, at], lambda q: o_send.at[s, q],
                   lambda q: o_recv.at[s, q], fold)

        def get(rows):
            v = here(s, a, rows)
            if A > 1:
                v = v + outb[s, near_a, rows]
            return v

        write(s, tails[s], packed, get)

    def finish_tail(s):
        rows = pl.ds(0, tails[s])

        def fold(x, y):
            yb[s, x, rows] = yb[s, x, rows] + yb[s, y, rows]

        arrive(b, B, lambda q: yb.at[s, q, rows], lambda q: y_send.at[s, q],
               lambda q: y_recv.at[s, q], fold)

        def get(rows):
            v = part[s, a * B + b, rows]
            if A > 1:
                v = v + zb[s, near_a, b, rows]
            if B > 1:
                v = v + yb[s, near, rows]
            return v

        write(s, 0, tails[s], get)

    lax.fori_loop(0, slots, link, 0)
    lax.fori_loop(0, C * tpp, ends, 0)
    sums[slots] = jnp.zeros((span, 2 * LANES), f32)

    def all_tails(s, now, dists):
        if A > 1:
            for dist in dists:
                tail_send(s, dist, now)

    every = range(A - 1, 0, -1)

    operand(0, me_row, 0)
    landed(0, mate, m_send.at[0], m_recv.at[0])
    operand(0, mate, 0)
    forward(0)
    for j in range(1, chips):
        operand(0, lax.rem(chip - j + chips, chips) * 2 + core, 0)
    for j in range(1, chips):
        src = lax.rem(chip - j + chips, chips) * 2 + (1 - core)
        landed(0, src, f_send.at[j - 1, 0], f_recv.at[j - 1, 0])
        operand(0, src, 0)
    tile_copy.wait()
    for blk in range(blocks):
        products(blk, LANES)
        pack(0, blk, 0)
        if blk == 0:
            all_tails(0, True, every)
            forward(1)
    for i in range(A):
        inner_send(0, i)
    forward(2)
    arrivals(1)
    operands(1, 0)
    for blk in range(blocks):
        products(blk, LANES)
        pack(1, blk, 0)
        if blk == 0:
            all_tails(1, True, every)
    for i in range(A):
        inner_send(1, i)
    forward(3)
    all_tails(0, False, list(every)[:-1])
    for s in (2, 3):
        arrivals(s)
        operands(s, (s - 2) * LANES)
    for blk in range(blocks):
        products(blk, 2 * LANES)
        for s in (2, 3):
            pack(s, blk, (s - 2) * LANES)
        if blk == 0:
            for i in range(A - 1):
                outer_step(0, i, True)
            all_tails(0, False, list(every)[-1:])
    for i in range(A):
        inner_send(2, i)
        inner_send(3, i)
    all_tails(1, False, every)
    for s in (0, 1):
        for i in range(A - 1):
            if s > 0:
                outer_step(s, i, True)
            outer_step(s, i, False)
    turn(0)
    turn(1)
    for i in range(A - 1):
        for s in (2, 3):
            outer_step(s, i, True)
            outer_step(s, i, False)
        if i < 2:
            finish(i)
    for s in range(min(2, A - 1), S):
        finish(s)
    for s in tailed:
        finish_tail(s)

    for sent in (directs.values(), mates.values(), forwards.values()):
        for cp in sent:
            cp.wait_send()
    for s in tailed:
        for dist in every:
            line(a, A, B, dist, lambda d, slot, to, *rest, s=s: tail_copy(s, d, slot, to).wait_send())
        for dist in range(B - 1, 0, -1):
            line(b, B, 1, dist, lambda t, slot, to, *rest, s=s: turn_copy(s, t, slot, to).wait_send())
    for s in range(S):
        for i in range(A):
            for dist in range(B - 1, 0, -1):
                def left(t, slot, to, *rest, s=s, d=pick(i)):
                    inner_copy(s, d, t, slot, to).wait_send()

                line(b, B, 1, dist, left)
        for i in range(A - 1):
            outer_copy(s, i)[-1].wait_send()


def body(vectors, tile_values, tile_rows, tile_cols, tile_count, degrees):
    R = lax.axis_size("row")
    C = lax.axis_size("col")
    piece, width = vectors.shape
    side = tile_values.shape[-1]
    slots = tile_values.shape[2]
    B = inner_size(C)
    A = C // B
    tpp = piece // side
    chips = R // 2
    dims = (R, A, B, piece, width, side, slots)
    vmem = pl.BlockSpec(memory_space=pltpu.VMEM)
    smem = pl.BlockSpec(memory_space=pltpu.SMEM)
    anywhere = pl.BlockSpec(memory_space=pl.ANY)
    dma = pltpu.SemaphoreType.DMA
    f32 = jnp.float32
    far = max(chips - 1, 1)
    S = SLICES
    packed = piece // S
    tails = tail_rows(packed)
    kinds = sum(1 for n in tails if n)
    return pl.pallas_call(
        functools.partial(kernel, dims),
        out_shape=jax.ShapeDtypeStruct((piece, width), f32),
        in_specs=[smem, smem, smem, anywhere, anywhere, anywhere],
        out_specs=vmem,
        scratch_shapes=[
            pltpu.VMEM((slots, side, side), tile_values.dtype),
            pltpu.VMEM((piece, width), f32),
            pltpu.VMEM((2, piece // LANES, LANES), jnp.int32),
            pltpu.VMEM((packed, LANES), f32),
            pltpu.VMEM((packed, LANES), f32),
            pltpu.VMEM((S, R, packed, LANES), f32),
            pltpu.VMEM((R * tpp, side, 2 * LANES), jnp.bfloat16),
            pltpu.VMEM((slots + 1, side * LANES * S // piece, 2 * LANES), f32),
            pltpu.VMEM((S, C, packed, LANES), f32),
            pltpu.VMEM((S, A, B + 1, packed, LANES), f32),
            pltpu.VMEM((S, A + 1, packed, LANES), f32),
            pltpu.VMEM((kinds, A + 1, B, max(tails), LANES), f32),
            pltpu.VMEM((kinds, B + 1, max(tails), LANES), f32),
            pltpu.SMEM((slots,), jnp.int32),
            pltpu.SMEM((C * tpp,), jnp.int32),
            dma, dma, dma((2,)),
            dma((far, S)), dma((far, S)),
            dma((S,)), dma((S,)),
            dma((far, S)), dma((far, S)),
            dma((S, A, B + 1)), dma((S, A, B + 1)),
            dma((S, A + 1)), dma((S, A + 1)),
            dma((kinds, A + 1)), dma((kinds, A + 1)),
            dma((kinds, B + 1)), dma((kinds, B + 1)),
        ],
        compiler_params=pltpu.CompilerParams(
            collective_id=0, has_side_effects=True, vmem_limit_bytes=67043328
        ),
    )(tile_rows, tile_cols, tile_count, vectors, degrees.reshape(-1, LANES), tile_values)


def solution(mesh):
    placed = (
        P(("col", "row"), None),
        P("row", "col", None, None, None),
        P("row", "col", None),
        P("row", "col", None),
        P("row", "col"),
        P(),
    )
    return jax.shard_map(
        body, mesh=mesh, in_specs=placed, out_specs=P(("row", "col"), None), check_vma=False
    )
```

```python
import functools

import jax
import jax.numpy as jnp
from jax import lax
from jax.experimental import pallas as pl
from jax.experimental.pallas import tpu as pltpu
from jax.sharding import PartitionSpec as P

MESH = pl.DeviceIdType.MESH
LANES = 128
SLICES = 4
CHUNK = 32


def inner_size(col_count):
    inner = 1
    while inner * inner * 4 <= col_count and col_count % (inner * 2) == 0:
        inner *= 2
    return inner


def sorted_table(count):
    return [sorted(range(count), key=lambda d: (-abs(d - i), -abs(2 * d - count + 1), -d)) for i in range(count)]


def slots_of(size):
    return size + 1 if size > 2 else 1


def outer_first(packed):
    e = packed // 16
    return [(0, 0, 2 * e), (0, 8 * e, 4 * e), (1, 0, 5 * e)]


def inner_first(packed):
    e = packed // 16
    return [(0, 2 * e, 2 * e), (0, 4 * e, 4 * e), (0, 12 * e, 4 * e), (1, 5 * e, 3 * e), (1, 8 * e, 8 * e),
            (2, 0, 8 * e), (3, 0, 8 * e), (2, 8 * e, 8 * e), (3, 8 * e, 8 * e)]


def outer_second(packed):
    e = packed // 16
    return [(0, 2 * e, 6 * e, (0, 1)), (0, 12 * e, 4 * e, (2,)), (1, 5 * e, 11 * e, (3, 4)),
            (2, 0, 8 * e, (5,)), (3, 0, 8 * e, (6,)), (2, 8 * e, 8 * e, (7,)), (3, 8 * e, 8 * e, (8,))]


def kernel(
    dims,
    rows_hbm, cols_hbm, count_hbm, vec_hbm, deg_hbm, tiles_hbm, out_ref,
    rows_s, cols_s, count_s,
    tiles_v, vec_v, deg_v, fin, fout, gath, rhs, sums, part, inb, outb, zb, yb, prev_s, last_s,
    list_sem, tile_sem, vec_sem, deg_sem, d_send, d_recv, m_send, m_recv, f_send, f_recv,
    i_send, i_recv, o_send, o_recv, z_send, z_recv, y_send, y_recv,
):
    R, A, B, piece, width, side, slots = dims
    C = A * B
    S = SLICES
    gw = width // S
    packed = piece // S
    tpp = piece // side
    halves = S // tpp
    blocks = S
    grain = packed // blocks
    span = side // blocks
    Z = outer_first(packed)
    Y = inner_first(packed)
    O = outer_second(packed)
    chips = R // 2
    me_row = lax.axis_index("row")
    me_col = lax.axis_index("col")
    chip, core = me_row // 2, me_row % 2
    mate = chip * 2 + (1 - core)
    a, b = me_col // B, me_col % B
    f32 = jnp.float32

    def rdma(src, dst, ssem, rsem, where):
        return pltpu.make_async_remote_copy(
            src_ref=src, dst_ref=dst, send_sem=ssem, recv_sem=rsem,
            device_id=where, device_id_type=MESH,
        )

    vec_copy = pltpu.make_async_copy(vec_hbm, vec_v, vec_sem)
    vec_copy.start()
    deg_n = piece // LANES
    deg_at = (me_col * R + me_row, me_row * C + me_col)
    deg_copies = []
    for i, at in enumerate(deg_at):
        cp = pltpu.make_async_copy(
            deg_hbm.at[pl.ds(pl.multiple_of(at * deg_n, deg_n), deg_n)], deg_v.at[i], deg_sem.at[i])
        cp.start()
        deg_copies.append(cp)
    list_copies = []
    for i, (src, dst) in enumerate(((rows_hbm, rows_s), (cols_hbm, cols_s), (count_hbm, count_s))):
        cp = pltpu.make_async_copy(src, dst, list_sem.at[i])
        cp.start()
        list_copies.append(cp)
    tile_copy = pltpu.make_async_copy(tiles_hbm.at[0, 0], tiles_v, tile_sem)
    tile_copy.start()

    barrier = pltpu.get_barrier_semaphore()

    def greet(where):
        pl.semaphore_signal(barrier, inc=1, device_id=where, device_id_type=MESH)

    greet({"row": mate})
    for j in range(1, chips):
        greet({"row": lax.rem(chip + j, chips) * 2 + core})
    conds = []
    if B > 1:
        conds += [(b > 0, me_col - 1), (b < B - 1, me_col + 1)]
    if A > 1:
        conds += [(a > 0, me_col - B), (a < A - 1, me_col + B)]
    for cond, other in conds:
        @pl.when(cond)
        def _(other=other):
            greet({"col": other})
    peers = jnp.int32(chips)
    for cond, other in conds:
        peers = peers + jnp.where(cond, 1, 0)

    group = lax.broadcasted_iota(jnp.int32, (CHUNK, LANES), 1) // gw
    odd = group % 2 == 1

    def place(q):
        u, h = q // halves, q % halves
        return u, h

    def first_row(blk, h):
        return (blk * halves + h) * grain

    def by_group(values):
        out = values[S - 1]
        for g in range(S - 2, -1, -1):
            out = jnp.where(group == g, values[g], out)
        return out

    def roll(x, steps):
        steps = steps % S
        return pltpu.roll(x, steps * gw, 1) if steps else x

    for cp in deg_copies:
        cp.wait()
    for i, ref in enumerate((fin, fout)):
        f = lax.rsqrt(deg_v[i].astype(f32))
        lane_at = lax.broadcasted_iota(jnp.int32, f.shape, 1) // grain
        for m in range(packed // LANES):
            rows = []
            for q in range(S):
                u, h = place(q)
                row = jnp.zeros((1, LANES), f32)
                for w in range(LANES // grain):
                    node = u * side + first_row(m * (LANES // grain) + w, h)
                    shift = (w * grain - node) % LANES
                    g = pltpu.roll(f, shift, 1) if shift else f
                    at = node // LANES
                    row = jnp.where(lane_at[:1] == w, g[at:at + 1, :], row)
                rows.append(jnp.broadcast_to(row, (gw, LANES)))
            ref[m * LANES:(m + 1) * LANES, :] = jnp.concatenate(rows, 0).T

    def pack_own(s):
        for blk in range(blocks):
            for c in range(0, grain, CHUNK):
                v = []
                for q in range(S):
                    u, h = place(q)
                    at = u * side + first_row(blk, h) + c
                    v.append(roll(vec_v[at:at + CHUNK], q - s))
                to = blk * grain + c
                gath[s, me_row, to:to + CHUNK] = by_group(v) * fin[to:to + CHUNK]

    def send_own(s):
        for j in range(1, chips):
            dst = lax.rem(chip + j, chips) * 2 + core
            cp = rdma(gath.at[s, me_row], gath.at[s, me_row],
                      d_send.at[j - 1], d_recv.at[j - 1, s], {"row": dst})
            cp.start()
        cp = rdma(gath.at[s, me_row], gath.at[s, me_row],
                  m_send.at[0], m_recv.at[s], {"row": mate})
        cp.start()

    vec_copy.wait()
    pack_own(0)
    pl.semaphore_wait(barrier, peers)
    send_own(0)
    for s in range(1, S):
        pack_own(s)
        send_own(s)

    def link(k, _):
        rk = rows_s[0, 0, k]
        v = jnp.int32(slots)
        for j in range(slots):
            v = jnp.where((rows_s[0, 0, j] == rk) & (j < k), j, v)
        prev_s[k] = v
        return 0

    def ends(r, _):
        v = jnp.int32(slots)
        for j in range(slots):
            v = jnp.where((rows_s[0, 0, j] == r) & (j < count), j, v)
        last_s[r] = v
        return 0

    def landed(s, r, ssem, rsem):
        rdma(gath.at[s, r], gath.at[s, r], ssem, rsem, {"row": mate}).wait_recv()

    low = group < S // 2

    def operand(s, r, lane):
        for blk in range(blocks):
            for c in range(0, grain, CHUNK):
                at = blk * grain + c
                x = gath[s, r, at:at + CHUNK]
                hi = x.astype(jnp.bfloat16).astype(f32)
                lo = x - hi
                same, swapped = jnp.where(odd, lo, hi), jnp.where(odd, hi, lo)
                t = (same, roll(swapped, 1), roll(same, 2), roll(swapped, 3))
                e, f = jnp.where(odd, t[1], t[0]), jnp.where(odd, t[3], t[2])
                g, k = jnp.where(odd, t[0], t[3]), jnp.where(odd, t[2], t[1])
                spread = (jnp.where(low, e, f), jnp.where(low, g, k),
                          jnp.where(low, f, e), jnp.where(low, k, g))
                for q in range(S):
                    u, h = place(q)
                    to = first_row(blk, h) + c
                    rhs[r * tpp + u, to:to + CHUNK, lane:lane + LANES] = spread[q].astype(jnp.bfloat16)

    def forward(s):
        for j in range(1, chips):
            src = lax.rem(chip - j + chips, chips) * 2 + core
            landed(s, src, d_send.at[j - 1], d_recv.at[j - 1, s])
            cp = rdma(gath.at[s, src], gath.at[s, src],
                      f_send.at[j - 1], f_recv.at[j - 1, s], {"row": mate})
            cp.start()

    def arrivals(s):
        landed(s, mate, m_send.at[0], m_recv.at[s])
        for j in range(1, chips):
            src = lax.rem(chip - j + chips, chips) * 2 + (1 - core)
            landed(s, src, f_send.at[j - 1], f_recv.at[j - 1, s])

    def operands(s, lane):
        def step(r, _):
            operand(s, r, lane)
            return 0

        lax.fori_loop(0, R, step, 0)

    def products(blk, lanes):
        def product(k, _):
            both = jnp.dot(tiles_v[k, blk * span:(blk + 1) * span], rhs[cols_s[0, 0, k], :, :lanes],
                           preferred_element_type=f32)
            sums[k, :, :lanes] = both + sums[prev_s[k], :, :lanes]
            return 0

        lax.fori_loop(0, slots, product, 0, unroll=True)

    def pack(s, blk, lane):
        def step(dest, _):
            for c in range(0, grain, CHUNK):
                v = []
                for q in range(S):
                    u, h = place(q)
                    at = h * grain + c
                    v.append(sums[last_s[dest * tpp + u], at:at + CHUNK, lane:lane + LANES])
                x = by_group(v)
                y = by_group([v[(g + 1) % S] for g in range(S)])
                at = blk * grain + c
                part[s, dest, at:at + CHUNK] = x + roll(y, 1)
            return 0

        lax.fori_loop(0, C, step, 0, unroll=8)

    order = sorted_table(A)

    def pick(i):
        v = jnp.int32(order[0][i])
        for n in range(1, A):
            v = jnp.where(a == n, order[n][i], v)
        return v

    def line(pos, size, stride, dist, action):
        for right in (True, False):
            t = pos + dist if right else pos - dist
            slot = 0 if size <= 2 else t + 1 if right else t
            to = me_col + stride if right else me_col - stride
            more = pos > 0 if right else pos < size - 1

            @pl.when((t < size) if right else (t >= 0))
            def _(t=t, slot=slot, to=to, more=more):
                action(t, slot, to, more, dist < size - 1)

    def arrive(pos, size, ref, ssem, rsem, fold):
        if size > 1:
            for cond, slot in ((pos > 0, pos + 1), (pos < size - 1, pos)):
                slot = 0 if size <= 2 else slot

                @pl.when(cond)
                def _(slot=slot):
                    rdma(ref(slot), ref(slot), ssem(slot), rsem(slot), {"row": mate}).wait_recv()
        if size > 2:
            @pl.when((pos > 0) & (pos < size - 1))
            def _():
                fold(pos + 1, pos)

    near = jnp.where(b > 0, b + 1, 0) if B > 2 else 0
    near_a = jnp.where(a > 0, a + 1, 0) if A > 2 else 0

    def inner_copy(n, d, t, slot, to):
        s, lo, size = Y[n]
        at = pl.ds(lo, size)
        return rdma(part.at[s, d * B + t, at], inb.at[s, d, slot, at],
                    i_send.at[d, slot], i_recv.at[n, d, slot], {"col": to})

    def inner_send(n, i):
        d = pick(i)
        s, lo, size = Y[n]
        at = pl.ds(lo, size)

        def action(t, slot, to, more, can):
            cp = inner_copy(n, d, t, slot, to)
            if can:
                @pl.when(more)
                def _():
                    cp.wait_recv()
                    part[s, d * B + t, at] = part[s, d * B + t, at] + inb[s, d, slot, at]
            cp.start()

        for dist in range(B - 1, 0, -1):
            line(b, B, 1, dist, action)

    def inner_done(n, d):
        s, lo, size = Y[n]
        at = pl.ds(lo, size)

        def fold(x, y):
            inb[s, d, x, at] = inb[s, d, x, at] + inb[s, d, y, at]

        arrive(b, B, lambda q: inb.at[s, d, q, at], lambda q: i_send.at[d, q],
               lambda q: i_recv.at[n, d, q], fold)

    def here(s, d, at):
        v = part[s, d * B + b, at]
        if B > 1:
            v = v + inb[s, d, near, at]
        return v

    def outer_copy(n, i):
        s, lo, size, _ = O[n]
        at = pl.ds(lo, size)
        d = pick(i)
        right = d > a
        slot = jnp.where(right, d + 1, d) if A > 2 else 0
        to = jnp.where(right, me_col + B, me_col - B)
        more = (right & (a > 0)) | (jnp.logical_not(right) & (a < A - 1))
        cp = rdma(part.at[s, d * B + b, at], outb.at[s, slot, at],
                  o_send.at[slot], o_recv.at[n, slot], {"col": to})
        return d, slot, more, cp

    def outer_now(n, i):
        d, slot, more, cp = outer_copy(n, i)
        s, lo, size, parts = O[n]
        at = pl.ds(lo, size)

        @pl.when(jnp.logical_not(more))
        def _():
            for p in parts:
                inner_done(p, d)
            part[s, d * B + b, at] = here(s, d, at)
            cp.start()

    def outer_later(n, i):
        d, slot, more, cp = outer_copy(n, i)
        s, lo, size, parts = O[n]
        at = pl.ds(lo, size)

        @pl.when(more)
        def _():
            for p in parts:
                inner_done(p, d)
            cp.wait_recv()
            part[s, d * B + b, at] = here(s, d, at) + outb[s, slot, at]
            cp.start()

    def tail_copy(n, d, slot, to):
        s, lo, size = Z[n]
        return rdma(part.at[s, pl.ds(d * B, B), pl.ds(lo, size)], zb.at[n, slot, :, pl.ds(0, size)],
                    z_send.at[slot], z_recv.at[n, slot], {"col": to})

    def tail_now(n):
        def action(d, slot, to, more, can):
            cp = tail_copy(n, d, slot, to)

            @pl.when(jnp.logical_not(more))
            def _():
                cp.start()

        for dist in range(A - 1, 0, -1):
            line(a, A, B, dist, action)

    def tail_later(n, dists):
        s, lo, size = Z[n]

        def action(d, slot, to, more, can):
            cp = tail_copy(n, d, slot, to)

            @pl.when(more)
            def _():
                cp.wait_recv()
                for t in range(B):
                    at = pl.ds(lo, size)
                    part[s, d * B + t, at] = part[s, d * B + t, at] + zb[n, slot, t, :size]
                cp.start()

        for dist in dists:
            line(a, A, B, dist, action)

    def turn_copy(n, t, slot, to):
        s, lo, size = Z[n]
        return rdma(part.at[s, a * B + t, pl.ds(lo, size)], yb.at[n, slot, pl.ds(0, size)],
                    y_send.at[slot], y_recv.at[n, slot], {"col": to})

    def turn(n):
        s, lo, size = Z[n]
        at = pl.ds(lo, size)

        def fold(x, y):
            zb[n, x, :, :size] = zb[n, x, :, :size] + zb[n, y, :, :size]

        arrive(a, A, lambda q: zb.at[n, q, :, pl.ds(0, size)], lambda q: z_send.at[q],
               lambda q: z_recv.at[n, q], fold)

        def action(t, slot, to, more, can):
            cp = turn_copy(n, t, slot, to)
            v = part[s, a * B + t, at]
            if A > 1:
                v = v + zb[n, near_a, t, :size]
            part[s, a * B + t, at] = v
            if can:
                @pl.when(more)
                def _():
                    cp.wait_recv()
                    part[s, a * B + t, at] = part[s, a * B + t, at] + yb[n, slot, :size]
            cp.start()

        for dist in range(B - 1, 0, -1):
            line(b, B, 1, dist, action)

    def write(s, lo, size, get):
        step = 16
        for at in range(lo, lo + size, step):
            blk, c = at // grain, at % grain
            total = get(at, step) * fout[at:at + step]
            for q in range(S):
                u, h = place(q)
                to = u * side + first_row(blk, h) + c
                out_ref[to:to + step, s * gw:(s + 1) * gw] = roll(total, s - q)[:, s * gw:(s + 1) * gw]

    def finish(n):
        s, lo, size, parts = O[n]
        at = pl.ds(lo, size)
        for p in parts:
            inner_done(p, a)
        if A > 1:
            def fold(x, y):
                outb[s, x, at] = outb[s, x, at] + outb[s, y, at]

            arrive(a, A, lambda q: outb.at[s, q, at], lambda q: o_send.at[q],
                   lambda q: o_recv.at[n, q], fold)

        def get(first, step):
            v = here(s, a, pl.ds(first, step))
            if A > 1:
                v = v + outb[s, near_a, first:first + step]
            return v

        write(s, lo, size, get)

    def finish_tail(n):
        s, lo, size = Z[n]

        def fold(x, y):
            yb[n, x, :size] = yb[n, x, :size] + yb[n, y, :size]

        arrive(b, B, lambda q: yb.at[n, q, pl.ds(0, size)], lambda q: y_send.at[q],
               lambda q: y_recv.at[n, q], fold)

        def get(first, step):
            v = part[s, a * B + b, first:first + step]
            at = first - lo
            if A > 1:
                v = v + zb[n, near_a, b, at:at + step]
            if B > 1:
                v = v + yb[n, near, at:at + step]
            return v

        write(s, lo, size, get)

    for cp in list_copies:
        cp.wait()
    count = count_s[0, 0]
    lax.fori_loop(0, slots, link, 0)
    lax.fori_loop(0, C * tpp, ends, 0)
    sums[slots] = jnp.zeros((span, 2 * LANES), f32)

    every = range(A)
    hops = range(A - 1)

    def inner_all(n):
        for i in every:
            inner_send(n, i)

    operand(0, me_row, 0)
    landed(0, mate, m_send.at[0], m_recv.at[0])
    operand(0, mate, 0)
    forward(0)
    for j in range(1, chips):
        operand(0, lax.rem(chip - j + chips, chips) * 2 + core, 0)
    for j in range(1, chips):
        src = lax.rem(chip - j + chips, chips) * 2 + (1 - core)
        landed(0, src, f_send.at[j - 1], f_recv.at[j - 1, 0])
        operand(0, src, 0)
    tile_copy.wait()
    def block(blk, lanes, first):
        products(blk, lanes)
        for n in range(lanes // LANES):
            pack(first + n, blk, n * LANES)

    block(0, LANES, 0)
    tail_now(0)
    inner_all(0)
    block(1, LANES, 0)
    inner_all(1)
    forward(1)
    block(2, LANES, 0)
    tail_now(1)
    block(3, LANES, 0)
    inner_all(2)
    forward(2)
    arrivals(1)
    operands(1, 0)
    block(0, LANES, 1)
    block(1, LANES, 1)
    tail_now(2)
    inner_all(3)
    block(2, LANES, 1)
    block(3, LANES, 1)
    inner_all(4)
    forward(3)
    far, near_hop = range(A - 2, 1, -1), range(min(1, A - 2), 0, -1)
    tail_later(0, far)
    for i in hops:
        outer_now(0, i)
    tail_later(1, far)
    for s in (2, 3):
        arrivals(s)
        operands(s, (s - 2) * LANES)
    for i in hops:
        outer_now(1, i)
    tail_later(0, near_hop)
    tail_later(1, near_hop)
    tail_later(2, far)
    block(0, 2 * LANES, 2)
    block(1, 2 * LANES, 2)
    inner_send(5, 0)
    inner_send(6, 0)
    block(2, 2 * LANES, 2)
    block(3, 2 * LANES, 2)
    inner_send(7, 0)
    inner_send(8, 0)
    for i in range(1, A):
        for n in (5, 6, 7, 8):
            inner_send(n, i)
    tail_later(2, near_hop)
    for i in hops:
        outer_now(2, i)
    for n in (0, 1, 2):
        for i in list(range(A - 3)) + list(range(A - 2, max(A - 4, -1), -1)):
            outer_later(n, i)
    last = (3, 4, 5, 6)
    now = [(n, i) for i in hops for n in last]
    later = sorted(now, key=lambda v: (max(v[1] - (A - 4), 0) * 2 + 0.1 * v[1] + 4 * min(v[1], A - 4) + last.index(v[0])))
    for k, (x, y) in enumerate(zip(now, later)):
        outer_now(*x)
        outer_later(*y)
        if k == 3:
            for n in range(len(Z)):
                turn(n)
            finish(0)
            finish(1)
        if k == 7:
            finish(2)
    for n in last:
        finish(n)
    for n in range(len(Z)):
        finish_tail(n)

    def all_sent(rows, sem):
        at = out_ref.at[pl.ds(0, rows)]
        rdma(at, at, sem, sem, {"row": mate}).wait_send()

    for j in range(1, chips):
        all_sent(piece, d_send.at[j - 1])
        all_sent(piece, f_send.at[j - 1])
    all_sent(piece, m_send.at[0])
    turned = sum(size for _, _, size in Z)
    for dist in range(A - 1, 0, -1):
        line(a, A, B, dist, lambda d, slot, *rest: all_sent(B * turned, z_send.at[slot]))
    for dist in range(B - 1, 0, -1):
        line(b, B, 1, dist, lambda t, slot, *rest: all_sent(turned, y_send.at[slot]))
    for d in range(A):
        for dist in range(B - 1, 0, -1):
            line(b, B, 1, dist, lambda t, slot, *rest, d=d: all_sent(piece - turned, i_send.at[d, slot]))
    for dist in range(A - 1, 0, -1):
        line(a, A, B, dist, lambda d, slot, *rest: all_sent(piece - turned, o_send.at[slot]))


def body(vectors, tile_values, tile_rows, tile_cols, tile_count, degrees):
    R = lax.axis_size("row")
    C = lax.axis_size("col")
    piece, width = vectors.shape
    side = tile_values.shape[-1]
    slots = tile_values.shape[2]
    B = inner_size(C)
    A = C // B
    tpp = piece // side
    chips = R // 2
    dims = (R, A, B, piece, width, side, slots)
    vmem = pl.BlockSpec(memory_space=pltpu.VMEM)
    anywhere = pl.BlockSpec(memory_space=pl.ANY)
    dma = pltpu.SemaphoreType.DMA
    f32 = jnp.float32
    far = max(chips - 1, 1)
    S = SLICES
    packed = piece // S
    Z, Y = outer_first(packed), inner_first(packed)
    NO = len(outer_second(packed))
    along, over = slots_of(A), slots_of(B)
    NZ, NY, longest = len(Z), len(Y), max(n for _, _, n in Z)
    smem_i32 = lambda *shape: pltpu.SMEM(shape, jnp.int32)
    return pl.pallas_call(
        functools.partial(kernel, dims),
        out_shape=jax.ShapeDtypeStruct((piece, width), f32),
        in_specs=[anywhere] * 6,
        out_specs=vmem,
        scratch_shapes=[
            smem_i32(1, 1, slots), smem_i32(1, 1, slots), smem_i32(1, 1),
            pltpu.VMEM((slots, side, side), tile_values.dtype),
            pltpu.VMEM((piece, width), f32),
            pltpu.VMEM((2, piece // LANES, LANES), jnp.int32),
            pltpu.VMEM((packed, LANES), f32),
            pltpu.VMEM((packed, LANES), f32),
            pltpu.VMEM((S, R, packed, LANES), f32),
            pltpu.VMEM((R * tpp, side, 2 * LANES), jnp.bfloat16),
            pltpu.VMEM((slots + 1, side // S, 2 * LANES), f32),
            pltpu.VMEM((S, C, packed, LANES), f32),
            pltpu.VMEM((S, A, over, packed, LANES), f32),
            pltpu.VMEM((S, along, packed, LANES), f32),
            pltpu.VMEM((NZ, along, B, longest, LANES), f32),
            pltpu.VMEM((NZ, over, longest, LANES), f32),
            smem_i32(slots), smem_i32(C * tpp),
            dma((3,)), dma, dma, dma((2,)),
            dma((far,)), dma((far, S)),
            dma((1,)), dma((S,)),
            dma((far,)), dma((far, S)),
            dma((A, over)), dma((NY, A, over)),
            dma((along,)), dma((NO, along)),
            dma((along,)), dma((NZ, along)),
            dma((over,)), dma((NZ, over)),
        ],
        compiler_params=pltpu.CompilerParams(
            collective_id=0, has_side_effects=True, vmem_limit_bytes=67043328
        ),
    )(tile_rows, tile_cols, tile_count, vectors, degrees.reshape(-1, LANES), tile_values)


def solution(mesh):
    placed = (
        P(("col", "row"), None),
        P("row", "col", None, None, None),
        P("row", "col", None),
        P("row", "col", None),
        P("row", "col"),
        P(),
    )
    return jax.shard_map(
        body, mesh=mesh, in_specs=placed, out_specs=P(("row", "col"), None), check_vma=False
    )
```

```python
import functools

import jax
import jax.numpy as jnp
from jax import lax
from jax.experimental import pallas as pl
from jax.experimental.pallas import tpu as pltpu
from jax.sharding import PartitionSpec as P

MESH = pl.DeviceIdType.MESH
LANES = 128
SLICES = 4
CHUNK = 32


def inner_size(col_count):
    inner = 1
    while inner * inner * 4 <= col_count and col_count % (inner * 2) == 0:
        inner *= 2
    return inner


def sorted_table(count):
    return [sorted(range(count), key=lambda d: (-abs(d - i), -abs(2 * d - count + 1), -d)) for i in range(count)]


def slots_of(size):
    return size + 1 if size > 2 else 1


def outer_first(packed):
    e = packed // 16
    return [(0, 0, 2 * e), (0, 8 * e, 4 * e), (1, 0, 4 * e)]


def inner_first(packed):
    e = packed // 16
    return [(0, 2 * e, 2 * e), (0, 4 * e, 4 * e), (0, 12 * e, 4 * e), (1, 4 * e, 4 * e), (1, 8 * e, 8 * e),
            (2, 0, 8 * e), (3, 0, 8 * e), (2, 8 * e, 8 * e), (3, 8 * e, 8 * e)]


def outer_second(packed):
    e = packed // 16
    return [(0, 2 * e, 6 * e, (0, 1)), (0, 12 * e, 4 * e, (2,)), (1, 4 * e, 12 * e, (3, 4)),
            (2, 0, 8 * e, (5,)), (3, 0, 8 * e, (6,)), (2, 8 * e, 8 * e, (7,)), (3, 8 * e, 8 * e, (8,))]


def kernel(
    dims,
    rows_hbm, cols_hbm, count_hbm, vec_hbm, deg_hbm, tiles_hbm, out_ref,
    rows_s, cols_s, count_s,
    tiles_v, vec_v, deg_v, fin, fout, gath, rhs, sums, part, inb, outb, zb, yb, prev_s, last_s,
    list_sem, tile_sem, vec_sem, deg_sem, d_send, d_recv, m_send, m_recv, f_send, f_recv,
    i_send, i_recv, o_send, o_recv, z_send, z_recv, y_send, y_recv,
):
    R, A, B, piece, width, side, slots = dims
    C = A * B
    S = SLICES
    gw = width // S
    packed = piece // S
    tpp = piece // side
    halves = S // tpp
    blocks = S
    grain = packed // blocks
    span = side // blocks
    Z = outer_first(packed)
    Y = inner_first(packed)
    O = outer_second(packed)
    chips = R // 2
    me_row = lax.axis_index("row")
    me_col = lax.axis_index("col")
    chip, core = me_row // 2, me_row % 2
    mate = chip * 2 + (1 - core)
    a, b = me_col // B, me_col % B
    f32 = jnp.float32

    def rdma(src, dst, ssem, rsem, where):
        return pltpu.make_async_remote_copy(
            src_ref=src, dst_ref=dst, send_sem=ssem, recv_sem=rsem,
            device_id=where, device_id_type=MESH,
        )

    vec_copy = pltpu.make_async_copy(vec_hbm, vec_v, vec_sem)
    vec_copy.start()
    deg_n = piece // LANES
    deg_at = (me_col * R + me_row, me_row * C + me_col)
    deg_copies = []
    for i, at in enumerate(deg_at):
        cp = pltpu.make_async_copy(
            deg_hbm.at[pl.ds(pl.multiple_of(at * deg_n, deg_n), deg_n)], deg_v.at[i], deg_sem.at[i])
        cp.start()
        deg_copies.append(cp)
    list_copies = []
    for i, (src, dst) in enumerate(((rows_hbm, rows_s), (cols_hbm, cols_s), (count_hbm, count_s))):
        cp = pltpu.make_async_copy(src, dst, list_sem.at[i])
        cp.start()
        list_copies.append(cp)
    tile_copy = pltpu.make_async_copy(tiles_hbm.at[0, 0], tiles_v, tile_sem)
    tile_copy.start()

    barrier = pltpu.get_barrier_semaphore()

    def greet(where):
        pl.semaphore_signal(barrier, inc=1, device_id=where, device_id_type=MESH)

    greet({"row": mate})
    for j in range(1, chips):
        greet({"row": lax.rem(chip + j, chips) * 2 + core})
    conds = []
    if B > 1:
        conds += [(b > 0, me_col - 1), (b < B - 1, me_col + 1)]
    if A > 1:
        conds += [(a > 0, me_col - B), (a < A - 1, me_col + B)]
    for cond, other in conds:
        @pl.when(cond)
        def _(other=other):
            greet({"col": other})
    peers = jnp.int32(chips)
    for cond, other in conds:
        peers = peers + jnp.where(cond, 1, 0)

    group = lax.broadcasted_iota(jnp.int32, (CHUNK, LANES), 1) // gw
    odd = group % 2 == 1

    def place(q):
        u, h = q // halves, q % halves
        return u, h

    def first_row(blk, h):
        return (blk * halves + h) * grain

    def by_group(values):
        out = values[S - 1]
        for g in range(S - 2, -1, -1):
            out = jnp.where(group == g, values[g], out)
        return out

    def roll(x, steps):
        steps = steps % S
        return pltpu.roll(x, steps * gw, 1) if steps else x

    for cp in deg_copies:
        cp.wait()
    for i, ref in enumerate((fin, fout)):
        f = lax.rsqrt(deg_v[i].astype(f32))
        lane_at = lax.broadcasted_iota(jnp.int32, f.shape, 1) // grain
        for m in range(packed // LANES):
            rows = []
            for q in range(S):
                u, h = place(q)
                row = jnp.zeros((1, LANES), f32)
                for w in range(LANES // grain):
                    node = u * side + first_row(m * (LANES // grain) + w, h)
                    shift = (w * grain - node) % LANES
                    g = pltpu.roll(f, shift, 1) if shift else f
                    at = node // LANES
                    row = jnp.where(lane_at[:1] == w, g[at:at + 1, :], row)
                rows.append(jnp.broadcast_to(row, (gw, LANES)))
            ref[m * LANES:(m + 1) * LANES, :] = jnp.concatenate(rows, 0).T

    def pack_own(s):
        for blk in range(blocks):
            for c in range(0, grain, CHUNK):
                v = []
                for q in range(S):
                    u, h = place(q)
                    at = u * side + first_row(blk, h) + c
                    v.append(roll(vec_v[at:at + CHUNK], q - s))
                to = blk * grain + c
                gath[s, me_row, to:to + CHUNK] = by_group(v) * fin[to:to + CHUNK]

    def send_own(s):
        for j in range(1, chips):
            dst = lax.rem(chip + j, chips) * 2 + core
            cp = rdma(gath.at[s, me_row], gath.at[s, me_row],
                      d_send.at[j - 1], d_recv.at[j - 1, s], {"row": dst})
            cp.start()
        cp = rdma(gath.at[s, me_row], gath.at[s, me_row],
                  m_send.at[0], m_recv.at[s], {"row": mate})
        cp.start()

    vec_copy.wait()
    pack_own(0)
    pl.semaphore_wait(barrier, peers)
    send_own(0)
    for s in range(1, S):
        pack_own(s)
        send_own(s)

    def link(k, _):
        rk = rows_s[0, 0, k]
        v = jnp.int32(slots)
        for j in range(slots):
            v = jnp.where((rows_s[0, 0, j] == rk) & (j < k), j, v)
        prev_s[k] = v
        return 0

    def ends(r, _):
        v = jnp.int32(slots)
        for j in range(slots):
            v = jnp.where((rows_s[0, 0, j] == r) & (j < count), j, v)
        last_s[r] = v
        return 0

    def landed(s, r, ssem, rsem):
        rdma(gath.at[s, r], gath.at[s, r], ssem, rsem, {"row": mate}).wait_recv()

    low = group < S // 2

    def operand(s, r, lane):
        for blk in range(blocks):
            for c in range(0, grain, CHUNK):
                at = blk * grain + c
                x = gath[s, r, at:at + CHUNK]
                hi = x.astype(jnp.bfloat16).astype(f32)
                lo = x - hi
                same, swapped = jnp.where(odd, lo, hi), jnp.where(odd, hi, lo)
                t = (same, roll(swapped, 1), roll(same, 2), roll(swapped, 3))
                e, f = jnp.where(odd, t[1], t[0]), jnp.where(odd, t[3], t[2])
                g, k = jnp.where(odd, t[0], t[3]), jnp.where(odd, t[2], t[1])
                spread = (jnp.where(low, e, f), jnp.where(low, g, k),
                          jnp.where(low, f, e), jnp.where(low, k, g))
                for q in range(S):
                    u, h = place(q)
                    to = first_row(blk, h) + c
                    rhs[r * tpp + u, to:to + CHUNK, lane:lane + LANES] = spread[q].astype(jnp.bfloat16)

    def forward(s):
        for j in range(1, chips):
            src = lax.rem(chip - j + chips, chips) * 2 + core
            landed(s, src, d_send.at[j - 1], d_recv.at[j - 1, s])
            cp = rdma(gath.at[s, src], gath.at[s, src],
                      f_send.at[j - 1], f_recv.at[j - 1, s], {"row": mate})
            cp.start()

    def arrivals(s):
        landed(s, mate, m_send.at[0], m_recv.at[s])
        for j in range(1, chips):
            src = lax.rem(chip - j + chips, chips) * 2 + (1 - core)
            landed(s, src, f_send.at[j - 1], f_recv.at[j - 1, s])

    def operands(s, lane):
        def step(r, _):
            operand(s, r, lane)
            return 0

        lax.fori_loop(0, R, step, 0)

    def products(blk, lanes):
        def product(k, _):
            both = jnp.dot(tiles_v[k, blk * span:(blk + 1) * span], rhs[cols_s[0, 0, k], :, :lanes],
                           preferred_element_type=f32)
            sums[k, :, :lanes] = both + sums[prev_s[k], :, :lanes]
            return 0

        lax.fori_loop(0, slots, product, 0, unroll=True)

    def pack(s, blk, lane):
        def step(dest, _):
            for c in range(0, grain, CHUNK):
                v = []
                for q in range(S):
                    u, h = place(q)
                    at = h * grain + c
                    v.append(sums[last_s[dest * tpp + u], at:at + CHUNK, lane:lane + LANES])
                x = by_group(v)
                y = by_group([v[(g + 1) % S] for g in range(S)])
                at = blk * grain + c
                part[s, dest, at:at + CHUNK] = x + roll(y, 1)
            return 0

        lax.fori_loop(0, C, step, 0, unroll=8)

    order = sorted_table(A)

    def pick(i):
        v = jnp.int32(order[0][i])
        for n in range(1, A):
            v = jnp.where(a == n, order[n][i], v)
        return v

    def line(pos, size, stride, dist, action):
        for right in (True, False):
            t = pos + dist if right else pos - dist
            slot = 0 if size <= 2 else t + 1 if right else t
            to = me_col + stride if right else me_col - stride
            more = pos > 0 if right else pos < size - 1

            @pl.when((t < size) if right else (t >= 0))
            def _(t=t, slot=slot, to=to, more=more):
                action(t, slot, to, more, dist < size - 1)

    def arrive(pos, size, ref, ssem, rsem, fold):
        if size > 1:
            for cond, slot in ((pos > 0, pos + 1), (pos < size - 1, pos)):
                slot = 0 if size <= 2 else slot

                @pl.when(cond)
                def _(slot=slot):
                    rdma(ref(slot), ref(slot), ssem(slot), rsem(slot), {"row": mate}).wait_recv()
        if size > 2:
            @pl.when((pos > 0) & (pos < size - 1))
            def _():
                fold(pos + 1, pos)

    near = jnp.where(b > 0, b + 1, 0) if B > 2 else 0
    near_a = jnp.where(a > 0, a + 1, 0) if A > 2 else 0

    def inner_copy(n, d, t, slot, to):
        s, lo, size = Y[n]
        at = pl.ds(lo, size)
        return rdma(part.at[s, d * B + t, at], inb.at[s, d, slot, at],
                    i_send.at[d, slot], i_recv.at[n, d, slot], {"col": to})

    def inner_send(n, i):
        d = pick(i)
        s, lo, size = Y[n]
        at = pl.ds(lo, size)

        def action(t, slot, to, more, can):
            cp = inner_copy(n, d, t, slot, to)
            if can:
                @pl.when(more)
                def _():
                    cp.wait_recv()
                    part[s, d * B + t, at] = part[s, d * B + t, at] + inb[s, d, slot, at]
            cp.start()

        for dist in range(B - 1, 0, -1):
            line(b, B, 1, dist, action)

    def inner_done(n, d):
        s, lo, size = Y[n]
        at = pl.ds(lo, size)

        def fold(x, y):
            inb[s, d, x, at] = inb[s, d, x, at] + inb[s, d, y, at]

        arrive(b, B, lambda q: inb.at[s, d, q, at], lambda q: i_send.at[d, q],
               lambda q: i_recv.at[n, d, q], fold)

    def here(s, d, at):
        v = part[s, d * B + b, at]
        if B > 1:
            v = v + inb[s, d, near, at]
        return v

    def outer_copy(n, i):
        s, lo, size, _ = O[n]
        at = pl.ds(lo, size)
        d = pick(i)
        right = d > a
        slot = jnp.where(right, d + 1, d) if A > 2 else 0
        to = jnp.where(right, me_col + B, me_col - B)
        more = (right & (a > 0)) | (jnp.logical_not(right) & (a < A - 1))
        cp = rdma(part.at[s, d * B + b, at], outb.at[s, slot, at],
                  o_send.at[slot], o_recv.at[n, slot], {"col": to})
        return d, slot, more, cp

    def outer_now(n, i):
        d, slot, more, cp = outer_copy(n, i)
        s, lo, size, parts = O[n]
        at = pl.ds(lo, size)

        @pl.when(jnp.logical_not(more))
        def _():
            for p in parts:
                inner_done(p, d)
            part[s, d * B + b, at] = here(s, d, at)
            cp.start()

    def outer_later(n, i):
        d, slot, more, cp = outer_copy(n, i)
        s, lo, size, parts = O[n]
        at = pl.ds(lo, size)

        @pl.when(more)
        def _():
            for p in parts:
                inner_done(p, d)
            cp.wait_recv()
            part[s, d * B + b, at] = here(s, d, at) + outb[s, slot, at]
            cp.start()

    def tail_copy(n, d, slot, to):
        s, lo, size = Z[n]
        return rdma(part.at[s, pl.ds(d * B, B), pl.ds(lo, size)], zb.at[n, slot, :, pl.ds(0, size)],
                    z_send.at[slot], z_recv.at[n, slot], {"col": to})

    def tail_now(n):
        def action(d, slot, to, more, can):
            cp = tail_copy(n, d, slot, to)

            @pl.when(jnp.logical_not(more))
            def _():
                cp.start()

        for dist in range(A - 1, 0, -1):
            line(a, A, B, dist, action)

    def tail_later(n, dists):
        s, lo, size = Z[n]

        def action(d, slot, to, more, can):
            cp = tail_copy(n, d, slot, to)

            @pl.when(more)
            def _():
                cp.wait_recv()
                for t in range(B):
                    at = pl.ds(lo, size)
                    part[s, d * B + t, at] = part[s, d * B + t, at] + zb[n, slot, t, :size]
                cp.start()

        for dist in dists:
            line(a, A, B, dist, action)

    def turn_copy(n, t, slot, to):
        s, lo, size = Z[n]
        return rdma(part.at[s, a * B + t, pl.ds(lo, size)], yb.at[n, slot, pl.ds(0, size)],
                    y_send.at[slot], y_recv.at[n, slot], {"col": to})

    def turn(n):
        s, lo, size = Z[n]
        at = pl.ds(lo, size)

        def fold(x, y):
            zb[n, x, :, :size] = zb[n, x, :, :size] + zb[n, y, :, :size]

        arrive(a, A, lambda q: zb.at[n, q, :, pl.ds(0, size)], lambda q: z_send.at[q],
               lambda q: z_recv.at[n, q], fold)

        def action(t, slot, to, more, can):
            cp = turn_copy(n, t, slot, to)
            v = part[s, a * B + t, at]
            if A > 1:
                v = v + zb[n, near_a, t, :size]
            part[s, a * B + t, at] = v
            if can:
                @pl.when(more)
                def _():
                    cp.wait_recv()
                    part[s, a * B + t, at] = part[s, a * B + t, at] + yb[n, slot, :size]
            cp.start()

        for dist in range(B - 1, 0, -1):
            line(b, B, 1, dist, action)

    def write(s, lo, size, get):
        step = 16
        for at in range(lo, lo + size, step):
            blk, c = at // grain, at % grain
            total = get(at, step) * fout[at:at + step]
            for q in range(S):
                u, h = place(q)
                to = u * side + first_row(blk, h) + c
                out_ref[to:to + step, s * gw:(s + 1) * gw] = roll(total, s - q)[:, s * gw:(s + 1) * gw]

    def finish(n):
        s, lo, size, parts = O[n]
        at = pl.ds(lo, size)
        for p in parts:
            inner_done(p, a)
        if A > 1:
            def fold(x, y):
                outb[s, x, at] = outb[s, x, at] + outb[s, y, at]

            arrive(a, A, lambda q: outb.at[s, q, at], lambda q: o_send.at[q],
                   lambda q: o_recv.at[n, q], fold)

        def get(first, step):
            v = here(s, a, pl.ds(first, step))
            if A > 1:
                v = v + outb[s, near_a, first:first + step]
            return v

        write(s, lo, size, get)

    def finish_tail(n):
        s, lo, size = Z[n]

        def fold(x, y):
            yb[n, x, :size] = yb[n, x, :size] + yb[n, y, :size]

        arrive(b, B, lambda q: yb.at[n, q, pl.ds(0, size)], lambda q: y_send.at[q],
               lambda q: y_recv.at[n, q], fold)

        def get(first, step):
            v = part[s, a * B + b, first:first + step]
            at = first - lo
            if A > 1:
                v = v + zb[n, near_a, b, at:at + step]
            if B > 1:
                v = v + yb[n, near, at:at + step]
            return v

        write(s, lo, size, get)

    for cp in list_copies:
        cp.wait()
    count = count_s[0, 0]
    lax.fori_loop(0, slots, link, 0)
    lax.fori_loop(0, C * tpp, ends, 0)
    sums[slots] = jnp.zeros((span, 2 * LANES), f32)

    every = range(A)
    hops = range(A - 1)

    def inner_all(n):
        for i in every:
            inner_send(n, i)

    operand(0, me_row, 0)
    landed(0, mate, m_send.at[0], m_recv.at[0])
    operand(0, mate, 0)
    forward(0)
    for j in range(1, chips):
        operand(0, lax.rem(chip - j + chips, chips) * 2 + core, 0)
    for j in range(1, chips):
        src = lax.rem(chip - j + chips, chips) * 2 + (1 - core)
        landed(0, src, f_send.at[j - 1], f_recv.at[j - 1, 0])
        operand(0, src, 0)
    tile_copy.wait()
    def block(blk, lanes, first):
        products(blk, lanes)
        for n in range(lanes // LANES):
            pack(first + n, blk, n * LANES)

    block(0, LANES, 0)
    tail_now(0)
    inner_all(0)
    block(1, LANES, 0)
    inner_all(1)
    forward(1)
    block(2, LANES, 0)
    tail_now(1)
    block(3, LANES, 0)
    inner_all(2)
    forward(2)
    arrivals(1)
    operands(1, 0)
    block(0, LANES, 1)
    block(1, LANES, 1)
    tail_now(2)
    inner_all(3)
    block(2, LANES, 1)
    block(3, LANES, 1)
    inner_all(4)
    forward(3)
    far, near_hop = range(A - 2, 1, -1), range(min(1, A - 2), 0, -1)
    tail_later(0, far)
    for i in hops:
        outer_now(0, i)
    tail_later(1, far)
    for s in (2, 3):
        arrivals(s)
        operands(s, (s - 2) * LANES)
    for i in hops:
        outer_now(1, i)
    block(0, 2 * LANES, 2)
    block(1, 2 * LANES, 2)
    inner_send(5, 0)
    inner_send(6, 0)
    tail_later(0, near_hop)
    tail_later(1, near_hop)
    tail_later(2, far)
    block(2, 2 * LANES, 2)
    block(3, 2 * LANES, 2)
    inner_send(7, 0)
    inner_send(8, 0)
    for i in range(1, A):
        for n in (5, 6, 7, 8):
            inner_send(n, i)
    tail_later(2, near_hop)
    for i in hops:
        outer_now(2, i)
    for n in (0, 1, 2):
        for i in list(range(A - 3)) + list(range(A - 2, max(A - 4, -1), -1)):
            outer_later(n, i)
    last = (3, 4, 5, 6)
    now = [(n, i) for i in hops for n in last]
    later = sorted(now, key=lambda v: (max(v[1] - (A - 4), 0) * 2 + 0.1 * v[1] + 4 * min(v[1], A - 4) + last.index(v[0])))
    for k, (x, y) in enumerate(zip(now, later)):
        outer_now(*x)
        outer_later(*y)
        if k == 3:
            for n in range(len(Z)):
                turn(n)
            finish(0)
            finish(1)
        if k == 7:
            finish(2)
    for n in last:
        finish(n)
    for n in range(len(Z)):
        finish_tail(n)

    def all_sent(rows, sem):
        at = out_ref.at[pl.ds(0, rows)]
        rdma(at, at, sem, sem, {"row": mate}).wait_send()

    for j in range(1, chips):
        all_sent(piece, d_send.at[j - 1])
        all_sent(piece, f_send.at[j - 1])
    all_sent(piece, m_send.at[0])
    turned = sum(size for _, _, size in Z)
    for dist in range(A - 1, 0, -1):
        line(a, A, B, dist, lambda d, slot, *rest: all_sent(B * turned, z_send.at[slot]))
    for dist in range(B - 1, 0, -1):
        line(b, B, 1, dist, lambda t, slot, *rest: all_sent(turned, y_send.at[slot]))
    for d in range(A):
        for dist in range(B - 1, 0, -1):
            line(b, B, 1, dist, lambda t, slot, *rest, d=d: all_sent(piece - turned, i_send.at[d, slot]))
    for dist in range(A - 1, 0, -1):
        line(a, A, B, dist, lambda d, slot, *rest: all_sent(piece - turned, o_send.at[slot]))


def body(vectors, tile_values, tile_rows, tile_cols, tile_count, degrees):
    R = lax.axis_size("row")
    C = lax.axis_size("col")
    piece, width = vectors.shape
    side = tile_values.shape[-1]
    slots = tile_values.shape[2]
    B = inner_size(C)
    A = C // B
    tpp = piece // side
    chips = R // 2
    dims = (R, A, B, piece, width, side, slots)
    vmem = pl.BlockSpec(memory_space=pltpu.VMEM)
    anywhere = pl.BlockSpec(memory_space=pl.ANY)
    dma = pltpu.SemaphoreType.DMA
    f32 = jnp.float32
    far = max(chips - 1, 1)
    S = SLICES
    packed = piece // S
    Z, Y = outer_first(packed), inner_first(packed)
    NO = len(outer_second(packed))
    along, over = slots_of(A), slots_of(B)
    NZ, NY, longest = len(Z), len(Y), max(n for _, _, n in Z)
    smem_i32 = lambda *shape: pltpu.SMEM(shape, jnp.int32)
    return pl.pallas_call(
        functools.partial(kernel, dims),
        out_shape=jax.ShapeDtypeStruct((piece, width), f32),
        in_specs=[anywhere] * 6,
        out_specs=vmem,
        scratch_shapes=[
            smem_i32(1, 1, slots), smem_i32(1, 1, slots), smem_i32(1, 1),
            pltpu.VMEM((slots, side, side), tile_values.dtype),
            pltpu.VMEM((piece, width), f32),
            pltpu.VMEM((2, piece // LANES, LANES), jnp.int32),
            pltpu.VMEM((packed, LANES), f32),
            pltpu.VMEM((packed, LANES), f32),
            pltpu.VMEM((S, R, packed, LANES), f32),
            pltpu.VMEM((R * tpp, side, 2 * LANES), jnp.bfloat16),
            pltpu.VMEM((slots + 1, side // S, 2 * LANES), f32),
            pltpu.VMEM((S, C, packed, LANES), f32),
            pltpu.VMEM((S, A, over, packed, LANES), f32),
            pltpu.VMEM((S, along, packed, LANES), f32),
            pltpu.VMEM((NZ, along, B, longest, LANES), f32),
            pltpu.VMEM((NZ, over, longest, LANES), f32),
            smem_i32(slots), smem_i32(C * tpp),
            dma((3,)), dma, dma, dma((2,)),
            dma((far,)), dma((far, S)),
            dma((1,)), dma((S,)),
            dma((far,)), dma((far, S)),
            dma((A, over)), dma((NY, A, over)),
            dma((along,)), dma((NO, along)),
            dma((along,)), dma((NZ, along)),
            dma((over,)), dma((NZ, over)),
        ],
        compiler_params=pltpu.CompilerParams(
            collective_id=0, has_side_effects=True, vmem_limit_bytes=67043328
        ),
    )(tile_rows, tile_cols, tile_count, vectors, degrees.reshape(-1, LANES), tile_values)


def solution(mesh):
    placed = (
        P(("col", "row"), None),
        P("row", "col", None, None, None),
        P("row", "col", None),
        P("row", "col", None),
        P("row", "col"),
        P(),
    )
    return jax.shard_map(
        body, mesh=mesh, in_specs=placed, out_specs=P(("row", "col"), None), check_vma=False
    )
```

```python
import functools

import jax
import jax.numpy as jnp
from jax import lax
from jax.experimental import pallas as pl
from jax.experimental.pallas import tpu as pltpu
from jax.sharding import PartitionSpec as P

MESH = pl.DeviceIdType.MESH
LANES = 128
SLICES = 4
CHUNK = 32


def inner_size(col_count):
    inner = 1
    while inner * inner * 4 <= col_count and col_count % (inner * 2) == 0:
        inner *= 2
    return inner


def sorted_table(count):
    return [sorted(range(count), key=lambda d: (-abs(d - i), -abs(2 * d - count + 1), -d)) for i in range(count)]


def slots_of(size):
    return size + 1 if size > 2 else 1


def outer_first(packed):
    e = packed // 16
    return [(0, 0, 2 * e), (0, 8 * e, 4 * e), (1, 0, 4 * e)]


def inner_first(packed):
    e = packed // 16
    return [(0, 2 * e, 2 * e), (0, 4 * e, 4 * e), (0, 12 * e, 4 * e), (1, 4 * e, 4 * e), (1, 8 * e, 8 * e),
            (2, 0, 8 * e), (3, 0, 8 * e), (2, 8 * e, 8 * e), (3, 8 * e, 8 * e)]


def outer_second(packed):
    e = packed // 16
    return [(0, 2 * e, 6 * e, (0, 1)), (0, 12 * e, 4 * e, (2,)), (1, 4 * e, 12 * e, (3, 4)),
            (2, 0, 8 * e, (5,)), (3, 0, 8 * e, (6,)), (2, 8 * e, 8 * e, (7,)), (3, 8 * e, 8 * e, (8,))]


def kernel(
    dims,
    rows_hbm, cols_hbm, count_hbm, vec_hbm, deg_hbm, tiles_hbm, out_ref,
    rows_s, cols_s, count_s,
    tiles_v, vec_v, deg_v, fin, fout, gath, rhs, sums, part, inb, outb, zb, yb, prev_s, last_s,
    list_sem, tile_sem, vec_sem, deg_sem, d_send, d_recv, m_send, m_recv, f_send, f_recv,
    i_send, i_recv, o_send, o_recv, z_send, z_recv, y_send, y_recv,
):
    R, A, B, piece, width, side, slots = dims
    C = A * B
    S = SLICES
    gw = width // S
    packed = piece // S
    tpp = piece // side
    halves = S // tpp
    blocks = S
    grain = packed // blocks
    span = side // blocks
    Z = outer_first(packed)
    Y = inner_first(packed)
    O = outer_second(packed)
    chips = R // 2
    me_row = lax.axis_index("row")
    me_col = lax.axis_index("col")
    chip, core = me_row // 2, me_row % 2
    mate = chip * 2 + (1 - core)
    a, b = me_col // B, me_col % B
    f32 = jnp.float32

    def rdma(src, dst, ssem, rsem, where):
        return pltpu.make_async_remote_copy(
            src_ref=src, dst_ref=dst, send_sem=ssem, recv_sem=rsem,
            device_id=where, device_id_type=MESH,
        )

    vec_copy = pltpu.make_async_copy(vec_hbm, vec_v, vec_sem)
    vec_copy.start()
    deg_n = piece // LANES
    deg_at = (me_col * R + me_row, me_row * C + me_col)
    deg_copies = []
    for i, at in enumerate(deg_at):
        cp = pltpu.make_async_copy(
            deg_hbm.at[pl.ds(pl.multiple_of(at * deg_n, deg_n), deg_n)], deg_v.at[i], deg_sem.at[i])
        cp.start()
        deg_copies.append(cp)
    list_copies = []
    for i, (src, dst) in enumerate(((rows_hbm, rows_s), (cols_hbm, cols_s), (count_hbm, count_s))):
        cp = pltpu.make_async_copy(src, dst, list_sem.at[i])
        cp.start()
        list_copies.append(cp)
    tile_copy = pltpu.make_async_copy(tiles_hbm.at[0, 0], tiles_v, tile_sem)
    tile_copy.start()

    barrier = pltpu.get_barrier_semaphore()

    def greet(where):
        pl.semaphore_signal(barrier, inc=1, device_id=where, device_id_type=MESH)

    greet({"row": mate})
    for j in range(1, chips):
        greet({"row": lax.rem(chip + j, chips) * 2 + core})
    conds = []
    if B > 1:
        conds += [(b > 0, me_col - 1), (b < B - 1, me_col + 1)]
    if A > 1:
        conds += [(a > 0, me_col - B), (a < A - 1, me_col + B)]
    for cond, other in conds:
        @pl.when(cond)
        def _(other=other):
            greet({"col": other})
    peers = jnp.int32(chips)
    for cond, other in conds:
        peers = peers + jnp.where(cond, 1, 0)

    group = lax.broadcasted_iota(jnp.int32, (CHUNK, LANES), 1) // gw
    odd = group % 2 == 1

    def place(q):
        u, h = q // halves, q % halves
        return u, h

    def first_row(blk, h):
        return (blk * halves + h) * grain

    def by_group(values):
        out = values[S - 1]
        for g in range(S - 2, -1, -1):
            out = jnp.where(group == g, values[g], out)
        return out

    def roll(x, steps):
        steps = steps % S
        return pltpu.roll(x, steps * gw, 1) if steps else x

    for cp in deg_copies:
        cp.wait()
    for i, ref in enumerate((fin, fout)):
        f = lax.rsqrt(deg_v[i].astype(f32))
        lane_at = lax.broadcasted_iota(jnp.int32, f.shape, 1) // grain
        for m in range(packed // LANES):
            rows = []
            for q in range(S):
                u, h = place(q)
                row = jnp.zeros((1, LANES), f32)
                for w in range(LANES // grain):
                    node = u * side + first_row(m * (LANES // grain) + w, h)
                    shift = (w * grain - node) % LANES
                    g = pltpu.roll(f, shift, 1) if shift else f
                    at = node // LANES
                    row = jnp.where(lane_at[:1] == w, g[at:at + 1, :], row)
                rows.append(jnp.broadcast_to(row, (gw, LANES)))
            ref[m * LANES:(m + 1) * LANES, :] = jnp.concatenate(rows, 0).T

    def pack_own(s):
        for blk in range(blocks):
            for c in range(0, grain, CHUNK):
                v = []
                for q in range(S):
                    u, h = place(q)
                    at = u * side + first_row(blk, h) + c
                    v.append(roll(vec_v[at:at + CHUNK], q - s))
                to = blk * grain + c
                gath[s, me_row, to:to + CHUNK] = by_group(v) * fin[to:to + CHUNK]

    def send_own(s):
        for j in range(1, chips):
            dst = lax.rem(chip + j, chips) * 2 + core
            cp = rdma(gath.at[s, me_row], gath.at[s, me_row],
                      d_send.at[j - 1], d_recv.at[j - 1, s], {"row": dst})
            cp.start()
        cp = rdma(gath.at[s, me_row], gath.at[s, me_row],
                  m_send.at[0], m_recv.at[s], {"row": mate})
        cp.start()

    vec_copy.wait()
    pack_own(0)
    pl.semaphore_wait(barrier, peers)
    send_own(0)
    for s in range(1, S):
        pack_own(s)
        send_own(s)

    def link(k, _):
        rk = rows_s[0, 0, k]
        v = jnp.int32(slots)
        for j in range(slots):
            v = jnp.where((rows_s[0, 0, j] == rk) & (j < k), j, v)
        prev_s[k] = v
        return 0

    def ends(r, _):
        v = jnp.int32(slots)
        for j in range(slots):
            v = jnp.where((rows_s[0, 0, j] == r) & (j < count), j, v)
        last_s[r] = v
        return 0

    def landed(s, r, ssem, rsem):
        rdma(gath.at[s, r], gath.at[s, r], ssem, rsem, {"row": mate}).wait_recv()

    low = group < S // 2

    def operand(s, r, lane):
        for blk in range(blocks):
            for c in range(0, grain, CHUNK):
                at = blk * grain + c
                x = gath[s, r, at:at + CHUNK]
                hi = x.astype(jnp.bfloat16).astype(f32)
                lo = x - hi
                same, swapped = jnp.where(odd, lo, hi), jnp.where(odd, hi, lo)
                t = (same, roll(swapped, 1), roll(same, 2), roll(swapped, 3))
                e, f = jnp.where(odd, t[1], t[0]), jnp.where(odd, t[3], t[2])
                g, k = jnp.where(odd, t[0], t[3]), jnp.where(odd, t[2], t[1])
                spread = (jnp.where(low, e, f), jnp.where(low, g, k),
                          jnp.where(low, f, e), jnp.where(low, k, g))
                for q in range(S):
                    u, h = place(q)
                    to = first_row(blk, h) + c
                    rhs[r * tpp + u, to:to + CHUNK, lane:lane + LANES] = spread[q].astype(jnp.bfloat16)

    def forward(s):
        for j in range(1, chips):
            src = lax.rem(chip - j + chips, chips) * 2 + core
            landed(s, src, d_send.at[j - 1], d_recv.at[j - 1, s])
            cp = rdma(gath.at[s, src], gath.at[s, src],
                      f_send.at[j - 1], f_recv.at[j - 1, s], {"row": mate})
            cp.start()

    def arrivals(s):
        landed(s, mate, m_send.at[0], m_recv.at[s])
        for j in range(1, chips):
            src = lax.rem(chip - j + chips, chips) * 2 + (1 - core)
            landed(s, src, f_send.at[j - 1], f_recv.at[j - 1, s])

    def operands(s, lane):
        def step(r, _):
            operand(s, r, lane)
            return 0

        lax.fori_loop(0, R, step, 0)

    def products(blk, lanes):
        def product(k, _):
            both = jnp.dot(tiles_v[k, blk * span:(blk + 1) * span], rhs[cols_s[0, 0, k], :, :lanes],
                           preferred_element_type=f32)
            sums[k, :, :lanes] = both + sums[prev_s[k], :, :lanes]
            return 0

        lax.fori_loop(0, slots, product, 0, unroll=True)

    def pack(s, blk, lane):
        def step(dest, _):
            for c in range(0, grain, CHUNK):
                v = []
                for q in range(S):
                    u, h = place(q)
                    at = h * grain + c
                    v.append(sums[last_s[dest * tpp + u], at:at + CHUNK, lane:lane + LANES])
                x = by_group(v)
                y = by_group([v[(g + 1) % S] for g in range(S)])
                at = blk * grain + c
                part[s, dest, at:at + CHUNK] = x + roll(y, 1)
            return 0

        lax.fori_loop(0, C, step, 0, unroll=8)

    order = sorted_table(A)

    def pick(i):
        v = jnp.int32(order[0][i])
        for n in range(1, A):
            v = jnp.where(a == n, order[n][i], v)
        return v

    def line(pos, size, stride, dist, action):
        for right in (True, False):
            t = pos + dist if right else pos - dist
            slot = 0 if size <= 2 else t + 1 if right else t
            to = me_col + stride if right else me_col - stride
            more = pos > 0 if right else pos < size - 1

            @pl.when((t < size) if right else (t >= 0))
            def _(t=t, slot=slot, to=to, more=more):
                action(t, slot, to, more, dist < size - 1)

    def arrive(pos, size, ref, ssem, rsem, fold):
        if size > 1:
            for cond, slot in ((pos > 0, pos + 1), (pos < size - 1, pos)):
                slot = 0 if size <= 2 else slot

                @pl.when(cond)
                def _(slot=slot):
                    rdma(ref(slot), ref(slot), ssem(slot), rsem(slot), {"row": mate}).wait_recv()
        if size > 2:
            @pl.when((pos > 0) & (pos < size - 1))
            def _():
                fold(pos + 1, pos)

    near = jnp.where(b > 0, b + 1, 0) if B > 2 else 0
    near_a = jnp.where(a > 0, a + 1, 0) if A > 2 else 0

    def inner_copy(n, d, t, slot, to):
        s, lo, size = Y[n]
        at = pl.ds(lo, size)
        return rdma(part.at[s, d * B + t, at], inb.at[s, d, slot, at],
                    i_send.at[d, slot], i_recv.at[n, d, slot], {"col": to})

    def inner_send(n, i):
        d = pick(i)
        s, lo, size = Y[n]
        at = pl.ds(lo, size)

        def action(t, slot, to, more, can):
            cp = inner_copy(n, d, t, slot, to)
            if can:
                @pl.when(more)
                def _():
                    cp.wait_recv()
                    part[s, d * B + t, at] = part[s, d * B + t, at] + inb[s, d, slot, at]
            cp.start()

        for dist in range(B - 1, 0, -1):
            line(b, B, 1, dist, action)

    def inner_done(n, d):
        s, lo, size = Y[n]
        at = pl.ds(lo, size)

        def fold(x, y):
            inb[s, d, x, at] = inb[s, d, x, at] + inb[s, d, y, at]

        arrive(b, B, lambda q: inb.at[s, d, q, at], lambda q: i_send.at[d, q],
               lambda q: i_recv.at[n, d, q], fold)

    def here(s, d, at):
        v = part[s, d * B + b, at]
        if B > 1:
            v = v + inb[s, d, near, at]
        return v

    def outer_copy(n, i):
        s, lo, size, _ = O[n]
        at = pl.ds(lo, size)
        d = pick(i)
        right = d > a
        slot = jnp.where(right, d + 1, d) if A > 2 else 0
        to = jnp.where(right, me_col + B, me_col - B)
        more = (right & (a > 0)) | (jnp.logical_not(right) & (a < A - 1))
        cp = rdma(part.at[s, d * B + b, at], outb.at[s, slot, at],
                  o_send.at[slot], o_recv.at[n, slot], {"col": to})
        return d, slot, more, cp

    def outer_now(n, i):
        d, slot, more, cp = outer_copy(n, i)
        s, lo, size, parts = O[n]
        at = pl.ds(lo, size)

        @pl.when(jnp.logical_not(more))
        def _():
            for p in parts:
                inner_done(p, d)
            part[s, d * B + b, at] = here(s, d, at)
            cp.start()

    def outer_later(n, i):
        d, slot, more, cp = outer_copy(n, i)
        s, lo, size, parts = O[n]
        at = pl.ds(lo, size)

        @pl.when(more)
        def _():
            for p in parts:
                inner_done(p, d)
            cp.wait_recv()
            part[s, d * B + b, at] = here(s, d, at) + outb[s, slot, at]
            cp.start()

    def tail_copy(n, d, slot, to):
        s, lo, size = Z[n]
        return rdma(part.at[s, pl.ds(d * B, B), pl.ds(lo, size)], zb.at[n, slot, :, pl.ds(0, size)],
                    z_send.at[slot], z_recv.at[n, slot], {"col": to})

    def tail_now(n):
        def action(d, slot, to, more, can):
            cp = tail_copy(n, d, slot, to)

            @pl.when(jnp.logical_not(more))
            def _():
                cp.start()

        for dist in range(A - 1, 0, -1):
            line(a, A, B, dist, action)

    def tail_later(n, dists):
        s, lo, size = Z[n]

        def action(d, slot, to, more, can):
            cp = tail_copy(n, d, slot, to)

            @pl.when(more)
            def _():
                cp.wait_recv()
                for t in range(B):
                    at = pl.ds(lo, size)
                    part[s, d * B + t, at] = part[s, d * B + t, at] + zb[n, slot, t, :size]
                cp.start()

        for dist in dists:
            line(a, A, B, dist, action)

    def turn_copy(n, t, slot, to):
        s, lo, size = Z[n]
        return rdma(part.at[s, a * B + t, pl.ds(lo, size)], yb.at[n, slot, pl.ds(0, size)],
                    y_send.at[slot], y_recv.at[n, slot], {"col": to})

    def turn(n):
        s, lo, size = Z[n]
        at = pl.ds(lo, size)

        def fold(x, y):
            zb[n, x, :, :size] = zb[n, x, :, :size] + zb[n, y, :, :size]

        arrive(a, A, lambda q: zb.at[n, q, :, pl.ds(0, size)], lambda q: z_send.at[q],
               lambda q: z_recv.at[n, q], fold)

        def action(t, slot, to, more, can):
            cp = turn_copy(n, t, slot, to)
            v = part[s, a * B + t, at]
            if A > 1:
                v = v + zb[n, near_a, t, :size]
            part[s, a * B + t, at] = v
            if can:
                @pl.when(more)
                def _():
                    cp.wait_recv()
                    part[s, a * B + t, at] = part[s, a * B + t, at] + yb[n, slot, :size]
            cp.start()

        for dist in range(B - 1, 0, -1):
            line(b, B, 1, dist, action)

    def write(s, lo, size, get):
        step = 16
        for at in range(lo, lo + size, step):
            blk, c = at // grain, at % grain
            total = get(at, step) * fout[at:at + step]
            for q in range(S):
                u, h = place(q)
                to = u * side + first_row(blk, h) + c
                out_ref[to:to + step, s * gw:(s + 1) * gw] = roll(total, s - q)[:, s * gw:(s + 1) * gw]

    def finish(n):
        s, lo, size, parts = O[n]
        at = pl.ds(lo, size)
        for p in parts:
            inner_done(p, a)
        if A > 1:
            def fold(x, y):
                outb[s, x, at] = outb[s, x, at] + outb[s, y, at]

            arrive(a, A, lambda q: outb.at[s, q, at], lambda q: o_send.at[q],
                   lambda q: o_recv.at[n, q], fold)

        def get(first, step):
            v = here(s, a, pl.ds(first, step))
            if A > 1:
                v = v + outb[s, near_a, first:first + step]
            return v

        write(s, lo, size, get)

    def finish_tail(n):
        s, lo, size = Z[n]

        def fold(x, y):
            yb[n, x, :size] = yb[n, x, :size] + yb[n, y, :size]

        arrive(b, B, lambda q: yb.at[n, q, pl.ds(0, size)], lambda q: y_send.at[q],
               lambda q: y_recv.at[n, q], fold)

        def get(first, step):
            v = part[s, a * B + b, first:first + step]
            at = first - lo
            if A > 1:
                v = v + zb[n, near_a, b, at:at + step]
            if B > 1:
                v = v + yb[n, near, at:at + step]
            return v

        write(s, lo, size, get)

    for cp in list_copies:
        cp.wait()
    count = count_s[0, 0]
    lax.fori_loop(0, slots, link, 0)
    lax.fori_loop(0, C * tpp, ends, 0)
    sums[slots] = jnp.zeros((span, 2 * LANES), f32)

    every = range(A)
    hops = range(A - 1)

    def inner_all(n):
        for i in every:
            inner_send(n, i)

    operand(0, me_row, 0)
    landed(0, mate, m_send.at[0], m_recv.at[0])
    operand(0, mate, 0)
    forward(0)
    for j in range(1, chips):
        operand(0, lax.rem(chip - j + chips, chips) * 2 + core, 0)
    for j in range(1, chips):
        src = lax.rem(chip - j + chips, chips) * 2 + (1 - core)
        landed(0, src, f_send.at[j - 1], f_recv.at[j - 1, 0])
        operand(0, src, 0)
    tile_copy.wait()
    def block(blk, lanes, first):
        products(blk, lanes)
        for n in range(lanes // LANES):
            pack(first + n, blk, n * LANES)

    block(0, LANES, 0)
    tail_now(0)
    inner_all(0)
    block(1, LANES, 0)
    inner_all(1)
    forward(1)
    block(2, LANES, 0)
    tail_now(1)
    block(3, LANES, 0)
    inner_all(2)
    forward(2)
    arrivals(1)
    operands(1, 0)
    block(0, LANES, 1)
    block(1, LANES, 1)
    tail_now(2)
    inner_all(3)
    block(2, LANES, 1)
    block(3, LANES, 1)
    inner_all(4)
    forward(3)
    far, near_hop = range(A - 2, 1, -1), range(min(1, A - 2), 0, -1)
    tail_later(0, far)
    for i in hops:
        outer_now(0, i)
    tail_later(1, far)
    for s in (2, 3):
        arrivals(s)
        operands(s, (s - 2) * LANES)
    for i in hops:
        outer_now(1, i)
    block(0, 2 * LANES, 2)
    block(1, 2 * LANES, 2)
    inner_send(5, 0)
    inner_send(6, 0)
    tail_later(0, near_hop)
    tail_later(1, near_hop)
    tail_later(2, far)
    block(2, 2 * LANES, 2)
    block(3, 2 * LANES, 2)
    inner_send(7, 0)
    inner_send(8, 0)
    for i in range(1, A):
        for n in (5, 6, 7, 8):
            inner_send(n, i)
    tail_later(2, near_hop)
    for i in hops:
        outer_now(2, i)
    lag = lambda i: 0.3 if i == A - 2 else 1.2 if i == A - 3 else 0
    for n, i in sorted(((n, i) for n in (0, 1, 2) for i in hops), key=lambda v: v[0] + lag(v[1])):
        outer_later(n, i)
    last = (3, 4, 5, 6)
    now = [(n, i) for i in hops for n in last]
    later = sorted(now, key=lambda v: (max(v[1] - (A - 4), 0) * 2 + 0.1 * v[1] + 4 * min(v[1], A - 4) + last.index(v[0])))
    for k, (x, y) in enumerate(zip(now, later)):
        outer_now(*x)
        outer_later(*y)
        if k == 6:
            for n in range(len(Z)):
                turn(n)
            finish(0)
            finish(1)
        if k == 9:
            finish(2)
    for n in last:
        finish(n)
    for n in range(len(Z)):
        finish_tail(n)

    def all_sent(rows, sem):
        at = out_ref.at[pl.ds(0, rows)]
        rdma(at, at, sem, sem, {"row": mate}).wait_send()

    for j in range(1, chips):
        all_sent(piece, d_send.at[j - 1])
        all_sent(piece, f_send.at[j - 1])
    all_sent(piece, m_send.at[0])
    turned = sum(size for _, _, size in Z)
    for dist in range(A - 1, 0, -1):
        line(a, A, B, dist, lambda d, slot, *rest: all_sent(B * turned, z_send.at[slot]))
    for dist in range(B - 1, 0, -1):
        line(b, B, 1, dist, lambda t, slot, *rest: all_sent(turned, y_send.at[slot]))
    for d in range(A):
        for dist in range(B - 1, 0, -1):
            line(b, B, 1, dist, lambda t, slot, *rest, d=d: all_sent(piece - turned, i_send.at[d, slot]))
    for dist in range(A - 1, 0, -1):
        line(a, A, B, dist, lambda d, slot, *rest: all_sent(piece - turned, o_send.at[slot]))


def body(vectors, tile_values, tile_rows, tile_cols, tile_count, degrees):
    R = lax.axis_size("row")
    C = lax.axis_size("col")
    piece, width = vectors.shape
    side = tile_values.shape[-1]
    slots = tile_values.shape[2]
    B = inner_size(C)
    A = C // B
    tpp = piece // side
    chips = R // 2
    dims = (R, A, B, piece, width, side, slots)
    vmem = pl.BlockSpec(memory_space=pltpu.VMEM)
    anywhere = pl.BlockSpec(memory_space=pl.ANY)
    dma = pltpu.SemaphoreType.DMA
    f32 = jnp.float32
    far = max(chips - 1, 1)
    S = SLICES
    packed = piece // S
    Z, Y = outer_first(packed), inner_first(packed)
    NO = len(outer_second(packed))
    along, over = slots_of(A), slots_of(B)
    NZ, NY, longest = len(Z), len(Y), max(n for _, _, n in Z)
    smem_i32 = lambda *shape: pltpu.SMEM(shape, jnp.int32)
    return pl.pallas_call(
        functools.partial(kernel, dims),
        out_shape=jax.ShapeDtypeStruct((piece, width), f32),
        in_specs=[anywhere] * 6,
        out_specs=vmem,
        scratch_shapes=[
            smem_i32(1, 1, slots), smem_i32(1, 1, slots), smem_i32(1, 1),
            pltpu.VMEM((slots, side, side), tile_values.dtype),
            pltpu.VMEM((piece, width), f32),
            pltpu.VMEM((2, piece // LANES, LANES), jnp.int32),
            pltpu.VMEM((packed, LANES), f32),
            pltpu.VMEM((packed, LANES), f32),
            pltpu.VMEM((S, R, packed, LANES), f32),
            pltpu.VMEM((R * tpp, side, 2 * LANES), jnp.bfloat16),
            pltpu.VMEM((slots + 1, side // S, 2 * LANES), f32),
            pltpu.VMEM((S, C, packed, LANES), f32),
            pltpu.VMEM((S, A, over, packed, LANES), f32),
            pltpu.VMEM((S, along, packed, LANES), f32),
            pltpu.VMEM((NZ, along, B, longest, LANES), f32),
            pltpu.VMEM((NZ, over, longest, LANES), f32),
            smem_i32(slots), smem_i32(C * tpp),
            dma((3,)), dma, dma, dma((2,)),
            dma((far,)), dma((far, S)),
            dma((1,)), dma((S,)),
            dma((far,)), dma((far, S)),
            dma((A, over)), dma((NY, A, over)),
            dma((along,)), dma((NO, along)),
            dma((along,)), dma((NZ, along)),
            dma((over,)), dma((NZ, over)),
        ],
        compiler_params=pltpu.CompilerParams(
            collective_id=0, has_side_effects=True, vmem_limit_bytes=67043328
        ),
    )(tile_rows, tile_cols, tile_count, vectors, degrees.reshape(-1, LANES), tile_values)


def solution(mesh):
    placed = (
        P(("col", "row"), None),
        P("row", "col", None, None, None),
        P("row", "col", None),
        P("row", "col", None),
        P("row", "col"),
        P(),
    )
    return jax.shard_map(
        body, mesh=mesh, in_specs=placed, out_specs=P(("row", "col"), None), check_vma=False
    )
```
